256 devices in a mesh: expert: 64 (over z_hi, y, x, core), dp: 4 (over z_lo).
Axes of the slice: x: 4, y: 4, z: 8 (z_hi: 2, z_lo: 4; z = z_hi * 4 + z_lo), core: 2. Of those that a mesh axis runs over, the one named last changes fastest.
Arguments:
- tokens: bfloat16 [8192, 4096], P('expert'), may hold values from -6 to 6
- cotangent: bfloat16 [8192, 4096], P('expert'), may hold values from -3 to 3
- gate_weight: bfloat16 [64, 768, 4096], P('expert', 'dp'), may hold values from -0.09375 to 0.09375
- up_weight: bfloat16 [64, 768, 4096], P('expert', 'dp'), may hold values from -0.09375 to 0.09375
- down_weight: bfloat16 [64, 768, 4096], P('expert', 'dp'), may hold values from -0.21875 to 0.21875
- expert_ids: int32 [8192, 4], P('expert'), may hold values from 0 to 63, all different within a row; in each aligned block of 128 rows (0 to 127, 128 to 255, ...) at most 10 rows name the same one
- gates: bfloat16 [8192, 4], P('expert'), may hold values from 0.049804688 to 0.59765625
- swap_flags: int32 [32], replicated, may hold values 0 or 1
Outputs:
- input_grad: bfloat16 [8192, 4096], P('expert', 'dp')
- gate_grad: bfloat16 [8192, 4], P('expert')
- gate_weight_grad: bfloat16 [64, 768, 4096], P('expert', 'dp')
- up_weight_grad: bfloat16 [64, 768, 4096], P('expert', 'dp')
- down_weight_grad: bfloat16 [64, 768, 4096], P('expert', 'dp')
The draws below stay inside these ranges and needn't reach their ends.
Inputs may be any that keep to these rules, and one draw needn't show every extreme that they name: `expert_ids`: each row names 4 different experts. Among the rows of one device no expert is named more than 10 times, and in every draw some expert is named exactly 10 times by the rows of some device.
All inputs are finite; a program needn't handle non-finite values.
Results may differ from the reference program's by a relative error of at most 0.011.
Values may be sent and summed in bfloat16 or wider, within the bound.
A program may use at most 128 MiB of HBM per device.

```python
import math
import jax
import jax.numpy as jnp
import numpy as np
from jax import lax

D = 4096
FF = 768
TOP = 4
TOK_DEV = 128
EXPERTS = 64
TOKENS = 8192
CAPACITY = 10
N_EXPERT = 64


def place_ends(values, own_key, smallest, high):
    place = [jax.random.randint(jax.random.fold_in(own_key, axis), (), 0, length) for axis, length in enumerate(values.shape)]
    longest = values.shape.index(max(values.shape))
    beside = place[:longest] + [(place[longest] + 1) % values.shape[longest]] + place[longest + 1:]
    return values.at[tuple(place)].set(smallest).at[tuple(beside)].set(high)


def block_levels(key, extent, pieces, least, top_value):
    def one(dim, shards_of):
        steps = jax.random.uniform(jax.random.fold_in(jax.random.fold_in(key, 6), dim), (shards_of,), jnp.float32, least / len(pieces), top_value / len(pieces))
        return jnp.repeat(jnp.exp(steps), extent[dim] // shards_of).reshape((-1,) + (1,) * (len(extent) - dim - 1))

    factor_of = one(*pieces[0])
    for cut in pieces[1:]:
        factor_of = factor_of * one(*cut)
    return factor_of


def shared_out(stream_key, own, number, rows, amount, top, bound, lean):
    sequence = jax.random.permutation(stream_key, amount)
    crowded, ordinary = load_shares(amount, rows * top, bound, lean, True), load_shares(amount, rows * top, bound, lean, False)
    places = jnp.arange(amount)

    def named(tallies, rotation):
        used = int((tallies > 0).sum())
        fixed = max(1, used // 4)
        moved = fixed + (places - fixed + rotation * (used - fixed)) % max(1, amount - fixed)
        return jnp.zeros((amount,), jnp.int32).at[sequence[jnp.where(places < fixed, places, moved)]].set(jnp.asarray(tallies, jnp.int32))

    tallies = jnp.where(number % 4 == 0, named(crowded, number // 4), named(ordinary, number - number // 4 - 1))
    mixed = jax.random.permutation(jax.random.fold_in(own, 3), amount)
    giver, taker = mixed[0:amount // 2 * 2:2], mixed[1:amount // 2 * 2:2]
    margin = jnp.minimum(tallies[giver] - 1, bound - tallies[taker]) // 2
    margin = jnp.where((giver == sequence[0]) | (taker == sequence[0]) | (tallies[taker] == 0), 0, jnp.maximum(margin, 0))
    moved = jax.random.randint(jax.random.fold_in(own, 4), (amount // 2,), 0, 1 << 20) % (margin + 1)
    tallies = tallies.at[giver].add(-moved).at[taker].add(moved)
    items = jnp.searchsorted(jnp.cumsum(tallies), jnp.arange(rows * top), side="right").astype(jnp.int32)
    table = items.reshape(top, rows).T
    table = table[jax.random.permutation(jax.random.fold_in(own, 1), rows)]
    rotation = jax.random.randint(jax.random.fold_in(own, 2), (rows, 1), 0, top)
    return jnp.take_along_axis(table, (jnp.arange(top)[None, :] + rotation) % top, axis=1)


def load_shares(amount, total, most, skew, full):
    portions = [(1 << 20) // math.isqrt(grade ** skew) + 1 for grade in range(1, amount + 1)]
    largest = most if full else min(most, max(-(-total // amount), total * portions[0] // sum(portions)))
    least = 1 if total - largest >= amount - 1 else 0
    given, rest = [largest] + [least] * (amount - 1), total - largest - least * (amount - 1)
    while rest > 0:
        free = [i for i in range(1, amount) if given[i] < largest] or [i for i in range(1, amount) if given[i] < most]
        pool, budget = sum([portions[i] for i in free]), rest
        for i in free:
            extra = min(most - given[i], max(1, budget * portions[i] // pool), rest)
            given[i] = given[i] + extra
            rest = rest - extra
    return np.array(given)


def normal_values(rng, extent, width, most, shards=(), kind=jnp.bfloat16):
    gain = block_levels(rng, extent, shards, -0.22, 0.18) if shards else 1.0
    result = jax.random.normal(rng, extent, jnp.float32) * width * gain
    return jnp.minimum(jnp.maximum(result, -most), most).astype(kind)


def setup_inputs(seed: int = 0) -> dict:
    splits = jax.random.split(jax.random.key(seed), 9)
    tokens = normal_values(splits[0], (TOKENS, D), 1.0, 6.0, ((0, 64),))
    cotangent = normal_values(splits[1], (TOKENS, D), 0.5, 3.0, ((0, 64),))
    gate_weight = normal_values(splits[2], (EXPERTS, FF, D), D ** -0.5, 0.09375, ((0, 64), (1, 4)))
    up_weight = normal_values(splits[3], (EXPERTS, FF, D), D ** -0.5, 0.09375, ((0, 64), (1, 4)))
    down_weight = normal_values(splits[4], (EXPERTS, FF, D), FF ** -0.5, 0.21875, ((0, 64), (1, 4)))
    expert_ids_keys = jax.random.split(jax.random.fold_in(splits[5], 1), TOKENS // TOK_DEV)
    expert_ids_turns = jax.random.permutation(jax.random.fold_in(splits[5], 3), TOKENS // TOK_DEV)
    expert_ids = jax.vmap(lambda own, number: shared_out(jax.random.fold_in(splits[5], 2), own, number, TOK_DEV, EXPERTS, TOP, CAPACITY, 2))(expert_ids_keys, expert_ids_turns).reshape((TOKENS, TOP))
    gates = jnp.clip(jnp.exp(math.log(0.59765625) - 2.4849066 * jax.random.uniform(splits[6], (TOKENS, TOP), jnp.float32) ** block_levels(splits[6], (TOKENS, TOP), ((0, 64),), -0.2, 0.2)), 0.049804688, 0.59765625).astype(jnp.bfloat16)
    swap_flags = place_ends((jax.random.randint(splits[7], (EXPERTS // 2,), 0, 2) < 1).astype(jnp.int32), jax.random.fold_in(splits[7], 1), 0, 1)
    return dict(tokens=tokens, cotangent=cotangent, gate_weight=gate_weight, up_weight=up_weight, down_weight=down_weight, expert_ids=expert_ids, gates=gates, swap_flags=swap_flags)


def expert_pass(x_rows, dy_rows, gate_rows, w_gate, w_up, w_down):
    pre_gate = lax.dot_general(x_rows, w_gate, (((1,), (1,)), ((), ())), preferred_element_type=jnp.float32)
    pre_up = lax.dot_general(x_rows, w_up, (((1,), (1,)), ((), ())), preferred_element_type=jnp.float32)
    sigma = jax.nn.sigmoid(pre_gate)
    active = pre_gate * sigma
    hidden = (active * pre_up).astype(jnp.bfloat16)
    back = lax.dot_general(dy_rows, w_down, (((1,), (1,)), ((), ())), preferred_element_type=jnp.float32)
    score = jnp.sum(hidden.astype(jnp.float32) * back, axis=1)
    grad_hidden = gate_rows.astype(jnp.float32)[:, None] * back
    slope = sigma * (1.0 + pre_gate * (1.0 - sigma))
    grad_gate = (grad_hidden * pre_up * slope).astype(jnp.bfloat16)
    grad_up = (grad_hidden * active).astype(jnp.bfloat16)
    input_rows = jnp.dot(grad_gate, w_gate, preferred_element_type=jnp.float32)
    input_rows = input_rows + jnp.dot(grad_up, w_up, preferred_element_type=jnp.float32)
    scaled = gate_rows[:, None] * dy_rows
    grad_wgate = lax.dot_general(grad_gate, x_rows, (((0,), (0,)), ((), ())), preferred_element_type=jnp.float32)
    grad_wup = lax.dot_general(grad_up, x_rows, (((0,), (0,)), ((), ())), preferred_element_type=jnp.float32)
    grad_wdown = lax.dot_general(hidden, scaled, (((0,), (0,)), ((), ())), preferred_element_type=jnp.float32)
    return (grad_wgate.astype(jnp.bfloat16), grad_wup.astype(jnp.bfloat16), grad_wdown.astype(jnp.bfloat16),
            input_rows.astype(jnp.bfloat16), score)


def reference(tokens, cotangent, gate_weight, up_weight, down_weight, expert_ids, gates, swap_flags):
    copies = TOKENS * TOP
    flat_ids = expert_ids.reshape(-1).astype(jnp.int32)
    flat_gates = gates.reshape(-1)
    sender = (jnp.arange(copies) // (TOK_DEV * TOP)).astype(jnp.int32)
    blocked = flat_ids.reshape(N_EXPERT, TOK_DEV * TOP)
    onehot = (blocked[:, :, None] == jnp.arange(EXPERTS, dtype=jnp.int32)[None, None, :]).astype(jnp.int32)
    earlier = jnp.cumsum(onehot, axis=1) - onehot
    position = jnp.sum(earlier * onehot, axis=2).reshape(-1).astype(jnp.int32)
    row_index = (sender * CAPACITY + position).astype(jnp.int32)
    table = jnp.zeros((EXPERTS, N_EXPERT * CAPACITY), jnp.int32)
    table = table.at[flat_ids, row_index].set(jnp.arange(copies, dtype=jnp.int32) + 1)

    def per_expert(packed):
        w_gate, w_up, w_down, source = packed
        filled = source > 0
        copy_index = jnp.maximum(source - 1, 0).astype(jnp.int32)
        token_index = (copy_index // TOP).astype(jnp.int32)
        x_rows = jnp.where(filled[:, None], tokens[token_index], 0)
        dy_rows = jnp.where(filled[:, None], cotangent[token_index], 0)
        gate_rows = jnp.where(filled, flat_gates[copy_index], 0)
        return expert_pass(x_rows, dy_rows, gate_rows, w_gate, w_up, w_down)

    grad_wgate, grad_wup, grad_wdown, input_rows, scores = lax.map(
        per_expert, (gate_weight, up_weight, down_weight, table))
    per_copy = input_rows[flat_ids, row_index].reshape(TOKENS, TOP, D)
    input_grad = jnp.sum(per_copy.astype(jnp.float32), axis=1).astype(jnp.bfloat16)
    gate_grad = scores[flat_ids, row_index].astype(jnp.bfloat16).reshape(TOKENS, TOP)
    half_axis = EXPERTS // 2
    slots = jnp.arange(EXPERTS, dtype=jnp.int32)
    pair_flag = swap_flags[slots % half_axis]
    holder = jnp.where(pair_flag == 1, (slots + half_axis) % EXPERTS, slots).astype(jnp.int32)
    return input_grad, gate_grad, grad_wgate[holder], grad_wup[holder], grad_wdown[holder]
```

```python
import jax
import jax.numpy as jnp
from jax import lax
from jax.sharding import PartitionSpec as P


def from_behind(value, axis, by):
    devices = lax.axis_size(axis)
    return lax.ppermute(value, axis, [(i, (i + by) % devices) for i in range(devices)])


def pair_lookup(experts, pair_flags, half_axis):
    match = experts[:, None] % half_axis == jnp.arange(half_axis, dtype=jnp.int32)[None, :]
    return jnp.sum(jnp.where(match, pair_flags[None, :], 0), axis=1)


def shards(tokens, cotangent, gate_weight, up_weight, down_weight, expert_ids, gates, swap_flags):
    expert_count = lax.axis_size("expert")
    half_axis = expert_count // 2
    my_slot = lax.axis_index("expert")
    row_count, model_width = tokens.shape
    routed = expert_ids.shape[1]
    capacity = row_count * routed * 5 // (4 * expert_count)
    groups = lax.axis_size("dp")
    quarter = model_width // groups
    own_flag = pair_lookup(jnp.reshape(my_slot, (1,)), swap_flags, half_axis)[0]
    flat_ids = expert_ids.reshape(-1)
    weights = (gate_weight, up_weight, down_weight)
    arrived = from_behind((gate_weight, up_weight, down_weight), "expert", half_axis)
    weights = tuple(
        (jnp.where(own_flag == 1, fresh, stay) for fresh, stay in zip(arrived, weights))
    )
    flipped = pair_lookup(flat_ids, swap_flags, half_axis)
    target = jnp.where(flipped == 1, (flat_ids + half_axis) % expert_count, flat_ids)
    copies = row_count * routed
    onehot = (target[:, None] == jnp.arange(expert_count, dtype=jnp.int32)[None, :]).astype(
        jnp.int32
    )
    earlier = jnp.cumsum(onehot, axis=0) - onehot
    position = jnp.sum(earlier * onehot, axis=1)
    buffer_index = target * capacity + position
    source = jnp.zeros((expert_count * capacity,), jnp.int32)
    source = source.at[buffer_index].set(jnp.arange(copies, dtype=jnp.int32) + 1)
    filled = source > 0
    copy_index = jnp.maximum(source - 1, 0)
    token_index = copy_index // routed
    x_buffer = jnp.where(filled[:, None], tokens[token_index], 0)
    dy_buffer = jnp.where(filled[:, None], cotangent[token_index], 0)
    gate_buffer = jnp.where(filled, gates.reshape(-1)[copy_index], 0)
    x_rows, dy_rows, gate_rows = (
        lax.all_to_all(x_buffer, "expert", split_axis=0, concat_axis=0, tiled=True),
        lax.all_to_all(dy_buffer, "expert", split_axis=0, concat_axis=0, tiled=True),
        lax.all_to_all(gate_buffer, "expert", split_axis=0, concat_axis=0, tiled=True),
    )
    w_gate = weights[0][0]
    w_up = weights[1][0]
    w_down = weights[2][0]
    contract_last = (((1,), (1,)), ((), ()))
    pre_gate = lax.dot_general(x_rows, w_gate, contract_last, preferred_element_type=jnp.float32)
    pre_up = lax.dot_general(x_rows, w_up, contract_last, preferred_element_type=jnp.float32)
    sigma = jax.nn.sigmoid(pre_gate)
    active = pre_gate * sigma
    hidden = (active * pre_up).astype(jnp.bfloat16)
    back = lax.dot_general(dy_rows, w_down, contract_last, preferred_element_type=jnp.float32)
    score_part = jnp.sum(hidden.astype(jnp.float32) * back, axis=1)
    grad_hidden = gate_rows.astype(jnp.float32)[:, None] * back
    slope = sigma * (1.0 + pre_gate * (1.0 - sigma))
    grad_gate = (grad_hidden * pre_up * slope).astype(jnp.bfloat16)
    grad_up = (grad_hidden * active).astype(jnp.bfloat16)
    input_part = jnp.dot(grad_gate, w_gate, preferred_element_type=jnp.float32)
    input_part = input_part + jnp.dot(grad_up, w_up, preferred_element_type=jnp.float32)
    scaled = gate_rows[:, None] * dy_rows
    contract_rows = (((0,), (0,)), ((), ()))
    grad_wgate = lax.dot_general(
        grad_gate, x_rows, contract_rows, preferred_element_type=jnp.float32
    )
    grad_wup = lax.dot_general(grad_up, x_rows, contract_rows, preferred_element_type=jnp.float32)
    grad_wdown = lax.dot_general(hidden, scaled, contract_rows, preferred_element_type=jnp.float32)
    score_cols = jnp.zeros((capacity * expert_count, groups, 128), jnp.float32)
    score_cols = score_cols.at[:, :, 0].set(score_part[:, None])
    packed = jnp.concatenate(
        [input_part.reshape(capacity * expert_count, groups, quarter), score_cols], axis=2
    ).astype(jnp.bfloat16)
    packed = packed.reshape(capacity * expert_count, groups * (quarter + 128))
    reduced = lax.psum_scatter(packed, "dp", scatter_dimension=1, tiled=True)
    back_rows = lax.all_to_all(reduced, "expert", split_axis=0, concat_axis=0, tiled=True)
    per_copy = back_rows[buffer_index].reshape(row_count, routed, quarter + 128)
    input_grad = jnp.sum(per_copy[:, :, :quarter].astype(jnp.float32), axis=1).astype(jnp.bfloat16)
    gate_grad = per_copy[:, :, quarter]
    gradients = (
        grad_wgate.astype(jnp.bfloat16)[None],
        grad_wup.astype(jnp.bfloat16)[None],
        grad_wdown.astype(jnp.bfloat16)[None],
    )
    return (input_grad, gate_grad, gradients[0], gradients[1], gradients[2])


def solution(mesh):
    placed = (
        P("expert", None),
        P("expert", None),
        P("expert", "dp", None),
        P("expert", "dp", None),
        P("expert", "dp", None),
        P("expert", None),
        P("expert", None),
        P(),
    )
    return jax.shard_map(
        shards,
        mesh=mesh,
        in_specs=placed,
        out_specs=(
            P("expert", "dp"),
            P("expert", None),
            P("expert", "dp", None),
            P("expert", "dp", None),
            P("expert", "dp", None),
        ),
        check_vma=False,
    )
```

```python
import jax
import jax.numpy as jnp
from jax import lax
from jax.sharding import PartitionSpec as P
from jax.experimental import pallas as pl
from jax.experimental.pallas import tpu as pltpu

MESH_IDS = pl.DeviceIdType.MESH


def dp_scatter_kernel(groups, src_ref, out_ref, landing, send_sem, recv_sem):
    me = lax.axis_index("dp")
    home = lax.axis_index("expert")
    width = out_ref.shape[1]
    barrier = pltpu.get_barrier_semaphore()
    for step in range(1, groups):
        peer = lax.rem(me + step, groups)
        pl.semaphore_signal(barrier, 1, device_id=(home, peer), device_id_type=MESH_IDS)
    pl.semaphore_wait(barrier, groups - 1)
    copies = []
    for step in range(1, groups):
        peer = lax.rem(me + step, groups)
        copy = pltpu.make_async_remote_copy(
            src_ref=src_ref.at[:, pl.ds(pl.multiple_of(peer * width, 128), width)],
            dst_ref=landing.at[step],
            send_sem=send_sem.at[step],
            recv_sem=recv_sem.at[step],
            device_id=(home, peer),
            device_id_type=MESH_IDS,
        )
        copy.start()
        copies.append(copy)
    for copy in copies:
        copy.wait()
    own = pl.multiple_of(me * width, 128)
    block = 64

    def body(i, carry):
        rows = pl.ds(pl.multiple_of(i * block, block), block)
        total = src_ref[rows, pl.ds(own, width)].astype(jnp.float32)
        for step in range(1, groups):
            total = total + landing[step, rows, :].astype(jnp.float32)
        out_ref[rows, :] = total.astype(out_ref.dtype)
        return carry

    lax.fori_loop(0, out_ref.shape[0] // block, body, 0)


def dp_scatter(packed, groups):
    rows, full = packed.shape
    width = full // groups
    return pl.pallas_call(
        lambda *refs: dp_scatter_kernel(groups, *refs),
        out_shape=jax.ShapeDtypeStruct((rows, width), packed.dtype),
        in_specs=[pl.BlockSpec(memory_space=pltpu.VMEM)],
        out_specs=pl.BlockSpec(memory_space=pltpu.VMEM),
        scratch_shapes=[
            pltpu.VMEM((groups, rows, width), packed.dtype),
            pltpu.SemaphoreType.DMA((groups,)),
            pltpu.SemaphoreType.DMA((groups,)),
        ],
        compiler_params=pltpu.CompilerParams(collective_id=0, has_side_effects=True),
    )(packed)


def from_behind(value, axis, by):
    devices = lax.axis_size(axis)
    return lax.ppermute(value, axis, [(i, (i + by) % devices) for i in range(devices)])


def pair_lookup(experts, pair_flags, half_axis):
    match = experts[:, None] % half_axis == jnp.arange(half_axis, dtype=jnp.int32)[None, :]
    return jnp.sum(jnp.where(match, pair_flags[None, :], 0), axis=1)


def shards(tokens, cotangent, gate_weight, up_weight, down_weight, expert_ids, gates, swap_flags):
    expert_count = lax.axis_size("expert")
    half_axis = expert_count // 2
    my_slot = lax.axis_index("expert")
    row_count, model_width = tokens.shape
    routed = expert_ids.shape[1]
    capacity = row_count * routed * 5 // (4 * expert_count)
    groups = lax.axis_size("dp")
    quarter = model_width // groups
    own_flag = pair_lookup(jnp.reshape(my_slot, (1,)), swap_flags, half_axis)[0]
    flat_ids = expert_ids.reshape(-1)
    weights = (gate_weight, up_weight, down_weight)
    arrived = from_behind((gate_weight, up_weight, down_weight), "expert", half_axis)
    weights = tuple(
        (jnp.where(own_flag == 1, fresh, stay) for fresh, stay in zip(arrived, weights))
    )
    flipped = pair_lookup(flat_ids, swap_flags, half_axis)
    target = jnp.where(flipped == 1, (flat_ids + half_axis) % expert_count, flat_ids)
    copies = row_count * routed
    onehot = (target[:, None] == jnp.arange(expert_count, dtype=jnp.int32)[None, :]).astype(
        jnp.int32
    )
    earlier = jnp.cumsum(onehot, axis=0) - onehot
    position = jnp.sum(earlier * onehot, axis=1)
    buffer_index = target * capacity + position
    source = jnp.zeros((expert_count * capacity,), jnp.int32)
    source = source.at[buffer_index].set(jnp.arange(copies, dtype=jnp.int32) + 1)
    filled = source > 0
    copy_index = jnp.maximum(source - 1, 0)
    token_index = copy_index // routed
    x_buffer = jnp.where(filled[:, None], tokens[token_index], 0)
    dy_buffer = jnp.where(filled[:, None], cotangent[token_index], 0)
    gate_buffer = jnp.where(filled, gates.reshape(-1)[copy_index], 0)
    x_rows, dy_rows, gate_rows = (
        lax.all_to_all(x_buffer, "expert", split_axis=0, concat_axis=0, tiled=True),
        lax.all_to_all(dy_buffer, "expert", split_axis=0, concat_axis=0, tiled=True),
        lax.all_to_all(gate_buffer, "expert", split_axis=0, concat_axis=0, tiled=True),
    )
    w_gate = weights[0][0]
    w_up = weights[1][0]
    w_down = weights[2][0]
    contract_last = (((1,), (1,)), ((), ()))
    pre_gate = lax.dot_general(x_rows, w_gate, contract_last, preferred_element_type=jnp.float32)
    pre_up = lax.dot_general(x_rows, w_up, contract_last, preferred_element_type=jnp.float32)
    sigma = jax.nn.sigmoid(pre_gate)
    active = pre_gate * sigma
    hidden = (active * pre_up).astype(jnp.bfloat16)
    back = lax.dot_general(dy_rows, w_down, contract_last, preferred_element_type=jnp.float32)
    score_part = jnp.sum(hidden.astype(jnp.float32) * back, axis=1)
    grad_hidden = gate_rows.astype(jnp.float32)[:, None] * back
    slope = sigma * (1.0 + pre_gate * (1.0 - sigma))
    grad_gate = (grad_hidden * pre_up * slope).astype(jnp.bfloat16)
    grad_up = (grad_hidden * active).astype(jnp.bfloat16)
    input_part = jnp.dot(grad_gate, w_gate, preferred_element_type=jnp.float32)
    input_part = input_part + jnp.dot(grad_up, w_up, preferred_element_type=jnp.float32)
    scaled = gate_rows[:, None] * dy_rows
    contract_rows = (((0,), (0,)), ((), ()))
    grad_wgate = lax.dot_general(
        grad_gate, x_rows, contract_rows, preferred_element_type=jnp.float32
    )
    grad_wup = lax.dot_general(grad_up, x_rows, contract_rows, preferred_element_type=jnp.float32)
    grad_wdown = lax.dot_general(hidden, scaled, contract_rows, preferred_element_type=jnp.float32)
    score_cols = jnp.zeros((capacity * expert_count, groups, 128), jnp.float32)
    score_cols = score_cols.at[:, :, 0].set(score_part[:, None])
    packed = jnp.concatenate(
        [input_part.reshape(capacity * expert_count, groups, quarter), score_cols], axis=2
    ).astype(jnp.bfloat16)
    packed = packed.reshape(capacity * expert_count, groups * (quarter + 128))
    reduced = dp_scatter(packed, groups)
    back_rows = lax.all_to_all(reduced, "expert", split_axis=0, concat_axis=0, tiled=True)
    per_copy = back_rows[buffer_index].reshape(row_count, routed, quarter + 128)
    input_grad = jnp.sum(per_copy[:, :, :quarter].astype(jnp.float32), axis=1).astype(jnp.bfloat16)
    gate_grad = per_copy[:, :, quarter]
    gradients = (
        grad_wgate.astype(jnp.bfloat16)[None],
        grad_wup.astype(jnp.bfloat16)[None],
        grad_wdown.astype(jnp.bfloat16)[None],
    )
    return (input_grad, gate_grad, gradients[0], gradients[1], gradients[2])


def solution(mesh):
    placed = (
        P("expert", None),
        P("expert", None),
        P("expert", "dp", None),
        P("expert", "dp", None),
        P("expert", "dp", None),
        P("expert", None),
        P("expert", None),
        P(),
    )
    return jax.shard_map(
        shards,
        mesh=mesh,
        in_specs=placed,
        out_specs=(
            P("expert", "dp"),
            P("expert", None),
            P("expert", "dp", None),
            P("expert", "dp", None),
            P("expert", "dp", None),
        ),
        check_vma=False,
    )
```

```python
import jax
import jax.numpy as jnp
from jax import lax
from jax.sharding import PartitionSpec as P
from jax.experimental import pallas as pl
from jax.experimental.pallas import tpu as pltpu

MESH_IDS = pl.DeviceIdType.MESH


def dp_scatter_kernel(groups, src_ref, out_ref, landing, send_sem, recv_sem):
    me = lax.axis_index("dp")
    home = lax.axis_index("expert")
    width = out_ref.shape[1]
    barrier = pltpu.get_barrier_semaphore()
    for step in range(1, groups):
        peer = lax.rem(me + step, groups)
        pl.semaphore_signal(barrier, 1, device_id=(home, peer), device_id_type=MESH_IDS)
    pl.semaphore_wait(barrier, groups - 1)
    copies = []
    for step in range(1, groups):
        peer = lax.rem(me + step, groups)
        copy = pltpu.make_async_remote_copy(
            src_ref=src_ref.at[:, pl.ds(pl.multiple_of(peer * width, 128), width)],
            dst_ref=landing.at[step],
            send_sem=send_sem.at[step],
            recv_sem=recv_sem.at[step],
            device_id=(home, peer),
            device_id_type=MESH_IDS,
        )
        copy.start()
        copies.append(copy)
    for copy in copies:
        copy.wait()
    own = pl.multiple_of(me * width, 128)
    block = 64

    def body(i, carry):
        rows = pl.ds(pl.multiple_of(i * block, block), block)
        total = src_ref[rows, pl.ds(own, width)].astype(jnp.float32)
        for step in range(1, groups):
            total = total + landing[step, rows, :].astype(jnp.float32)
        out_ref[rows, :] = total.astype(out_ref.dtype)
        return carry

    lax.fori_loop(0, out_ref.shape[0] // block, body, 0)


def dp_scatter(packed, groups):
    rows, full = packed.shape
    width = full // groups
    return pl.pallas_call(
        lambda *refs: dp_scatter_kernel(groups, *refs),
        out_shape=jax.ShapeDtypeStruct((rows, width), packed.dtype),
        in_specs=[pl.BlockSpec(memory_space=pltpu.VMEM)],
        out_specs=pl.BlockSpec(memory_space=pltpu.VMEM),
        scratch_shapes=[
            pltpu.VMEM((groups, rows, width), packed.dtype),
            pltpu.SemaphoreType.DMA((groups,)),
            pltpu.SemaphoreType.DMA((groups,)),
        ],
        compiler_params=pltpu.CompilerParams(collective_id=0, has_side_effects=True),
    )(packed)


def dispatch_kernel(count, src_ref, out_ref, local_sem, send_sem, recv_sem):
    me = lax.axis_index("expert")
    group = lax.axis_index("dp")
    barrier = pltpu.get_barrier_semaphore()

    def greet(step, carry):
        peer = lax.rem(me + step, count)
        pl.semaphore_signal(barrier, 1, device_id=(peer, group), device_id_type=MESH_IDS)
        return carry

    lax.fori_loop(1, count, greet, 0)
    pl.semaphore_wait(barrier, count - 1)
    local = pltpu.make_async_copy(src_ref.at[me], out_ref.at[me], local_sem)
    local.start()

    def describe(step):
        peer = lax.rem(me + step, count)
        return pltpu.make_async_remote_copy(
            src_ref=src_ref.at[peer],
            dst_ref=out_ref.at[me],
            send_sem=send_sem.at[step],
            recv_sem=recv_sem.at[step],
            device_id=(peer, group),
            device_id_type=MESH_IDS,
        )

    def launch(step, carry):
        describe(step).start()
        return carry

    def finish(step, carry):
        describe(step).wait()
        return carry

    lax.fori_loop(1, count, launch, 0)
    local.wait()
    lax.fori_loop(1, count, finish, 0)


def dispatch(buffer, count):
    return pl.pallas_call(
        lambda *refs: dispatch_kernel(count, *refs),
        out_shape=jax.ShapeDtypeStruct(buffer.shape, buffer.dtype),
        in_specs=[pl.BlockSpec(memory_space=pl.ANY)],
        out_specs=pl.BlockSpec(memory_space=pl.ANY),
        scratch_shapes=[
            pltpu.SemaphoreType.DMA(()),
            pltpu.SemaphoreType.DMA((count,)),
            pltpu.SemaphoreType.DMA((count,)),
        ],
        compiler_params=pltpu.CompilerParams(collective_id=1, has_side_effects=True),
    )(buffer)


def from_behind(value, axis, by):
    devices = lax.axis_size(axis)
    return lax.ppermute(value, axis, [(i, (i + by) % devices) for i in range(devices)])


def pair_lookup(experts, pair_flags, half_axis):
    match = experts[:, None] % half_axis == jnp.arange(half_axis, dtype=jnp.int32)[None, :]
    return jnp.sum(jnp.where(match, pair_flags[None, :], 0), axis=1)


def shards(tokens, cotangent, gate_weight, up_weight, down_weight, expert_ids, gates, swap_flags):
    expert_count = lax.axis_size("expert")
    half_axis = expert_count // 2
    my_slot = lax.axis_index("expert")
    row_count, model_width = tokens.shape
    routed = expert_ids.shape[1]
    capacity = row_count * routed * 5 // (4 * expert_count)
    groups = lax.axis_size("dp")
    quarter = model_width // groups
    own_flag = pair_lookup(jnp.reshape(my_slot, (1,)), swap_flags, half_axis)[0]
    flat_ids = expert_ids.reshape(-1)
    weights = (gate_weight, up_weight, down_weight)
    arrived = from_behind((gate_weight, up_weight, down_weight), "expert", half_axis)
    weights = tuple(
        (jnp.where(own_flag == 1, fresh, stay) for fresh, stay in zip(arrived, weights))
    )
    flipped = pair_lookup(flat_ids, swap_flags, half_axis)
    target = jnp.where(flipped == 1, (flat_ids + half_axis) % expert_count, flat_ids)
    copies = row_count * routed
    onehot = (target[:, None] == jnp.arange(expert_count, dtype=jnp.int32)[None, :]).astype(
        jnp.int32
    )
    earlier = jnp.cumsum(onehot, axis=0) - onehot
    position = jnp.sum(earlier * onehot, axis=1)
    buffer_index = target * capacity + position
    source = jnp.zeros((expert_count * capacity,), jnp.int32)
    source = source.at[buffer_index].set(jnp.arange(copies, dtype=jnp.int32) + 1)
    filled = source > 0
    copy_index = jnp.maximum(source - 1, 0)
    token_index = copy_index // routed
    x_buffer = jnp.where(filled[:, None], tokens[token_index], 0)
    dy_buffer = jnp.where(filled[:, None], cotangent[token_index], 0)
    gate_buffer = jnp.where(filled, gates.reshape(-1)[copy_index], 0)
    gate_cols = jnp.zeros((expert_count * capacity, 128), jnp.bfloat16).at[:, 0].set(gate_buffer)
    outgoing = jnp.concatenate([x_buffer, dy_buffer, gate_cols], axis=1)
    outgoing = outgoing.reshape(expert_count, capacity, 2 * model_width + 128)
    arrived_rows = dispatch(outgoing, expert_count).reshape(expert_count * capacity, -1)
    x_rows = arrived_rows[:, :model_width]
    dy_rows = arrived_rows[:, model_width : 2 * model_width]
    gate_rows = arrived_rows[:, 2 * model_width]
    w_gate = weights[0][0]
    w_up = weights[1][0]
    w_down = weights[2][0]
    contract_last = (((1,), (1,)), ((), ()))
    pre_gate = lax.dot_general(x_rows, w_gate, contract_last, preferred_element_type=jnp.float32)
    pre_up = lax.dot_general(x_rows, w_up, contract_last, preferred_element_type=jnp.float32)
    sigma = jax.nn.sigmoid(pre_gate)
    active = pre_gate * sigma
    hidden = (active * pre_up).astype(jnp.bfloat16)
    back = lax.dot_general(dy_rows, w_down, contract_last, preferred_element_type=jnp.float32)
    score_part = jnp.sum(hidden.astype(jnp.float32) * back, axis=1)
    grad_hidden = gate_rows.astype(jnp.float32)[:, None] * back
    slope = sigma * (1.0 + pre_gate * (1.0 - sigma))
    grad_gate = (grad_hidden * pre_up * slope).astype(jnp.bfloat16)
    grad_up = (grad_hidden * active).astype(jnp.bfloat16)
    input_part = jnp.dot(grad_gate, w_gate, preferred_element_type=jnp.float32)
    input_part = input_part + jnp.dot(grad_up, w_up, preferred_element_type=jnp.float32)
    scaled = gate_rows[:, None] * dy_rows
    contract_rows = (((0,), (0,)), ((), ()))
    grad_wgate = lax.dot_general(
        grad_gate, x_rows, contract_rows, preferred_element_type=jnp.float32
    )
    grad_wup = lax.dot_general(grad_up, x_rows, contract_rows, preferred_element_type=jnp.float32)
    grad_wdown = lax.dot_general(hidden, scaled, contract_rows, preferred_element_type=jnp.float32)
    score_cols = jnp.zeros((capacity * expert_count, groups, 128), jnp.float32)
    score_cols = score_cols.at[:, :, 0].set(score_part[:, None])
    packed = jnp.concatenate(
        [input_part.reshape(capacity * expert_count, groups, quarter), score_cols], axis=2
    ).astype(jnp.bfloat16)
    packed = packed.reshape(capacity * expert_count, groups * (quarter + 128))
    reduced = dp_scatter(packed, groups)
    back_rows = lax.all_to_all(reduced, "expert", split_axis=0, concat_axis=0, tiled=True)
    per_copy = back_rows[buffer_index].reshape(row_count, routed, quarter + 128)
    input_grad = jnp.sum(per_copy[:, :, :quarter].astype(jnp.float32), axis=1).astype(jnp.bfloat16)
    gate_grad = per_copy[:, :, quarter]
    gradients = (
        grad_wgate.astype(jnp.bfloat16)[None],
        grad_wup.astype(jnp.bfloat16)[None],
        grad_wdown.astype(jnp.bfloat16)[None],
    )
    return (input_grad, gate_grad, gradients[0], gradients[1], gradients[2])


def solution(mesh):
    placed = (
        P("expert", None),
        P("expert", None),
        P("expert", "dp", None),
        P("expert", "dp", None),
        P("expert", "dp", None),
        P("expert", None),
        P("expert", None),
        P(),
    )
    return jax.shard_map(
        shards,
        mesh=mesh,
        in_specs=placed,
        out_specs=(
            P("expert", "dp"),
            P("expert", None),
            P("expert", "dp", None),
            P("expert", "dp", None),
            P("expert", "dp", None),
        ),
        check_vma=False,
    )
```

```python
import jax
import jax.numpy as jnp
from jax import lax
from jax.sharding import PartitionSpec as P
from jax.experimental import pallas as pl
from jax.experimental.pallas import tpu as pltpu

MESH_IDS = pl.DeviceIdType.MESH


def dp_scatter_kernel(groups, src_ref, out_ref, landing, send_sem, recv_sem):
    me = lax.axis_index("dp")
    home = lax.axis_index("expert")
    width = out_ref.shape[1]
    barrier = pltpu.get_barrier_semaphore()
    for step in range(1, groups):
        peer = lax.rem(me + step, groups)
        pl.semaphore_signal(barrier, 1, device_id=(home, peer), device_id_type=MESH_IDS)
    pl.semaphore_wait(barrier, groups - 1)
    copies = []
    for step in range(1, groups):
        peer = lax.rem(me + step, groups)
        copy = pltpu.make_async_remote_copy(
            src_ref=src_ref.at[:, pl.ds(pl.multiple_of(peer * width, 128), width)],
            dst_ref=landing.at[step],
            send_sem=send_sem.at[step],
            recv_sem=recv_sem.at[step],
            device_id=(home, peer),
            device_id_type=MESH_IDS,
        )
        copy.start()
        copies.append(copy)
    for copy in copies:
        copy.wait()
    own = pl.multiple_of(me * width, 128)
    block = 64

    def body(i, carry):
        rows = pl.ds(pl.multiple_of(i * block, block), block)
        total = src_ref[rows, pl.ds(own, width)].astype(jnp.float32)
        for step in range(1, groups):
            total = total + landing[step, rows, :].astype(jnp.float32)
        out_ref[rows, :] = total.astype(out_ref.dtype)
        return carry

    lax.fori_loop(0, out_ref.shape[0] // block, body, 0)


def dp_scatter(packed, groups):
    rows, full = packed.shape
    width = full // groups
    return pl.pallas_call(
        lambda *refs: dp_scatter_kernel(groups, *refs),
        out_shape=jax.ShapeDtypeStruct((rows, width), packed.dtype),
        in_specs=[pl.BlockSpec(memory_space=pltpu.VMEM)],
        out_specs=pl.BlockSpec(memory_space=pltpu.VMEM),
        scratch_shapes=[
            pltpu.VMEM((groups, rows, width), packed.dtype),
            pltpu.SemaphoreType.DMA((groups,)),
            pltpu.SemaphoreType.DMA((groups,)),
        ],
        compiler_params=pltpu.CompilerParams(collective_id=0, has_side_effects=True),
    )(packed)


def dp_gather_kernel(groups, src_ref, out_ref, local_sem, send_sem, recv_sem):
    me = lax.axis_index("dp")
    home = lax.axis_index("expert")
    barrier = pltpu.get_barrier_semaphore()
    for step in range(1, groups):
        peer = lax.rem(me + step, groups)
        pl.semaphore_signal(barrier, 1, device_id=(home, peer), device_id_type=MESH_IDS)
    pl.semaphore_wait(barrier, groups - 1)
    copies = []
    for step in range(1, groups):
        peer = lax.rem(me + step, groups)
        copy = pltpu.make_async_remote_copy(
            src_ref=src_ref,
            dst_ref=out_ref.at[me],
            send_sem=send_sem.at[step],
            recv_sem=recv_sem.at[step],
            device_id=(home, peer),
            device_id_type=MESH_IDS,
        )
        copy.start()
        copies.append(copy)
    local = pltpu.make_async_copy(src_ref, out_ref.at[me], local_sem)
    local.start()
    local.wait()
    for copy in copies:
        copy.wait()


def dp_gather(chunk, groups):
    return pl.pallas_call(
        lambda *refs: dp_gather_kernel(groups, *refs),
        out_shape=jax.ShapeDtypeStruct((groups,) + chunk.shape, chunk.dtype),
        in_specs=[pl.BlockSpec(memory_space=pl.ANY)],
        out_specs=pl.BlockSpec(memory_space=pl.ANY),
        scratch_shapes=[
            pltpu.SemaphoreType.DMA(()),
            pltpu.SemaphoreType.DMA((groups,)),
            pltpu.SemaphoreType.DMA((groups,)),
        ],
        compiler_params=pltpu.CompilerParams(collective_id=2, has_side_effects=True),
    )(chunk)


def from_behind(value, axis, by):
    devices = lax.axis_size(axis)
    return lax.ppermute(value, axis, [(i, (i + by) % devices) for i in range(devices)])


def pair_lookup(experts, pair_flags, half_axis):
    match = experts[:, None] % half_axis == jnp.arange(half_axis, dtype=jnp.int32)[None, :]
    return jnp.sum(jnp.where(match, pair_flags[None, :], 0), axis=1)


def shards(tokens, cotangent, gate_weight, up_weight, down_weight, expert_ids, gates, swap_flags):
    expert_count = lax.axis_size("expert")
    half_axis = expert_count // 2
    my_slot = lax.axis_index("expert")
    row_count, model_width = tokens.shape
    routed = expert_ids.shape[1]
    capacity = row_count * routed * 5 // (4 * expert_count)
    groups = lax.axis_size("dp")
    quarter = model_width // groups
    own_flag = pair_lookup(jnp.reshape(my_slot, (1,)), swap_flags, half_axis)[0]
    flat_ids = expert_ids.reshape(-1)
    weights = (gate_weight, up_weight, down_weight)
    arrived = from_behind((gate_weight, up_weight, down_weight), "expert", half_axis)
    weights = tuple(
        (jnp.where(own_flag == 1, fresh, stay) for fresh, stay in zip(arrived, weights))
    )
    flipped = pair_lookup(flat_ids, swap_flags, half_axis)
    target = jnp.where(flipped == 1, (flat_ids + half_axis) % expert_count, flat_ids)
    copies = row_count * routed
    onehot = (target[:, None] == jnp.arange(expert_count, dtype=jnp.int32)[None, :]).astype(
        jnp.int32
    )
    earlier = jnp.cumsum(onehot, axis=0) - onehot
    position = jnp.sum(earlier * onehot, axis=1)
    buffer_index = target * capacity + position
    source = jnp.zeros((expert_count * capacity,), jnp.int32)
    source = source.at[buffer_index].set(jnp.arange(copies, dtype=jnp.int32) + 1)
    filled = source > 0
    copy_index = jnp.maximum(source - 1, 0)
    token_index = copy_index // routed
    my_group = lax.axis_index("dp")
    x_part = lax.dynamic_slice_in_dim(tokens, my_group * quarter, quarter, axis=1)
    dy_part = lax.dynamic_slice_in_dim(cotangent, my_group * quarter, quarter, axis=1)
    x_buffer = jnp.where(filled[:, None], x_part[token_index], 0)
    dy_buffer = jnp.where(filled[:, None], dy_part[token_index], 0)
    gate_buffer = jnp.where(filled, gates.reshape(-1)[copy_index], 0)
    gate_cols = jnp.zeros((expert_count * capacity, 128), jnp.bfloat16).at[:, 0].set(gate_buffer)
    outgoing = jnp.concatenate([x_buffer, dy_buffer, gate_cols], axis=1)
    arrived = lax.all_to_all(outgoing, "expert", split_axis=0, concat_axis=0, tiled=True)
    gathered = dp_gather(arrived, groups)
    x_rows = jnp.transpose(gathered[:, :, :quarter], (1, 0, 2)).reshape(-1, model_width)
    dy_rows = jnp.transpose(gathered[:, :, quarter : 2 * quarter], (1, 0, 2)).reshape(-1, model_width)
    gate_rows = gathered[0, :, 2 * quarter]
    w_gate = weights[0][0]
    w_up = weights[1][0]
    w_down = weights[2][0]
    contract_last = (((1,), (1,)), ((), ()))
    pre_gate = lax.dot_general(x_rows, w_gate, contract_last, preferred_element_type=jnp.float32)
    pre_up = lax.dot_general(x_rows, w_up, contract_last, preferred_element_type=jnp.float32)
    sigma = jax.nn.sigmoid(pre_gate)
    active = pre_gate * sigma
    hidden = (active * pre_up).astype(jnp.bfloat16)
    back = lax.dot_general(dy_rows, w_down, contract_last, preferred_element_type=jnp.float32)
    score_part = jnp.sum(hidden.astype(jnp.float32) * back, axis=1)
    grad_hidden = gate_rows.astype(jnp.float32)[:, None] * back
    slope = sigma * (1.0 + pre_gate * (1.0 - sigma))
    grad_gate = (grad_hidden * pre_up * slope).astype(jnp.bfloat16)
    grad_up = (grad_hidden * active).astype(jnp.bfloat16)
    input_part = jnp.dot(grad_gate, w_gate, preferred_element_type=jnp.float32)
    input_part = input_part + jnp.dot(grad_up, w_up, preferred_element_type=jnp.float32)
    scaled = gate_rows[:, None] * dy_rows
    contract_rows = (((0,), (0,)), ((), ()))
    grad_wgate = lax.dot_general(
        grad_gate, x_rows, contract_rows, preferred_element_type=jnp.float32
    )
    grad_wup = lax.dot_general(grad_up, x_rows, contract_rows, preferred_element_type=jnp.float32)
    grad_wdown = lax.dot_general(hidden, scaled, contract_rows, preferred_element_type=jnp.float32)
    score_cols = jnp.zeros((capacity * expert_count, groups, 128), jnp.float32)
    score_cols = score_cols.at[:, :, 0].set(score_part[:, None])
    packed = jnp.concatenate(
        [input_part.reshape(capacity * expert_count, groups, quarter), score_cols], axis=2
    ).astype(jnp.bfloat16)
    packed = packed.reshape(capacity * expert_count, groups * (quarter + 128))
    reduced = dp_scatter(packed, groups)
    back_rows = lax.all_to_all(reduced, "expert", split_axis=0, concat_axis=0, tiled=True)
    per_copy = back_rows[buffer_index].reshape(row_count, routed, quarter + 128)
    input_grad = jnp.sum(per_copy[:, :, :quarter].astype(jnp.float32), axis=1).astype(jnp.bfloat16)
    gate_grad = per_copy[:, :, quarter]
    gradients = (
        grad_wgate.astype(jnp.bfloat16)[None],
        grad_wup.astype(jnp.bfloat16)[None],
        grad_wdown.astype(jnp.bfloat16)[None],
    )
    return (input_grad, gate_grad, gradients[0], gradients[1], gradients[2])


def solution(mesh):
    placed = (
        P("expert", None),
        P("expert", None),
        P("expert", "dp", None),
        P("expert", "dp", None),
        P("expert", "dp", None),
        P("expert", None),
        P("expert", None),
        P(),
    )
    return jax.shard_map(
        shards,
        mesh=mesh,
        in_specs=placed,
        out_specs=(
            P("expert", "dp"),
            P("expert", None),
            P("expert", "dp", None),
            P("expert", "dp", None),
            P("expert", "dp", None),
        ),
        check_vma=False,
    )
```

```python
import jax
import jax.numpy as jnp
from jax import lax
from jax.sharding import PartitionSpec as P
from jax.experimental import pallas as pl
from jax.experimental.pallas import tpu as pltpu

MESH_IDS = pl.DeviceIdType.MESH


def dp_scatter_kernel(groups, src_ref, score_ref, out_ref, landing, score_in, send_sem, recv_sem):
    me = lax.axis_index("dp")
    home = lax.axis_index("expert")
    width = landing.shape[2]
    barrier = pltpu.get_barrier_semaphore()
    for step in range(1, groups):
        peer = lax.rem(me + step, groups)
        pl.semaphore_signal(barrier, 1, device_id=(home, peer), device_id_type=MESH_IDS)
    pl.semaphore_wait(barrier, groups - 1)
    copies = []
    for step in range(1, groups):
        peer = lax.rem(me + step, groups)
        for part, (source, target) in enumerate(
            ((src_ref.at[:, pl.ds(pl.multiple_of(peer * width, 128), width)], landing), (score_ref, score_in))
        ):
            copy = pltpu.make_async_remote_copy(
                src_ref=source,
                dst_ref=target.at[step],
                send_sem=send_sem.at[step, part],
                recv_sem=recv_sem.at[step, part],
                device_id=(home, peer),
                device_id_type=MESH_IDS,
            )
            copy.start()
            copies.append(copy)
    for copy in copies:
        copy.wait()
    own = pl.multiple_of(me * width, 128)
    block = 64

    def body(i, carry):
        rows = pl.ds(pl.multiple_of(i * block, block), block)
        total = src_ref[rows, pl.ds(own, width)].astype(jnp.float32)
        score = score_ref[rows, :]
        for step in range(1, groups):
            total = total + landing[step, rows, :].astype(jnp.float32)
            score = score + score_in[step, rows, :]
        out_ref[rows, pl.ds(0, width)] = total.astype(out_ref.dtype)
        out_ref[rows, pl.ds(width, 128)] = score.astype(out_ref.dtype)
        return carry

    lax.fori_loop(0, out_ref.shape[0] // block, body, 0)


def dp_scatter(partial, score, groups):
    rows, full = partial.shape
    width = full // groups
    return pl.pallas_call(
        lambda *refs: dp_scatter_kernel(groups, *refs),
        out_shape=jax.ShapeDtypeStruct((rows, width + 128), partial.dtype),
        in_specs=[pl.BlockSpec(memory_space=pltpu.VMEM)] * 2,
        out_specs=pl.BlockSpec(memory_space=pltpu.VMEM),
        scratch_shapes=[
            pltpu.VMEM((groups, rows, width), partial.dtype),
            pltpu.VMEM((groups, rows, 128), score.dtype),
            pltpu.SemaphoreType.DMA((groups, 2)),
            pltpu.SemaphoreType.DMA((groups, 2)),
        ],
        compiler_params=pltpu.CompilerParams(collective_id=0, has_side_effects=True),
    )(partial, score)


def dp_gather_kernel(groups, width, src_ref, x_ref, dy_ref, local_sem, send_sem, recv_sem):
    me = lax.axis_index("dp")
    home = lax.axis_index("expert")
    barrier = pltpu.get_barrier_semaphore()
    for step in range(1, groups):
        peer = lax.rem(me + step, groups)
        pl.semaphore_signal(barrier, 1, device_id=(home, peer), device_id_type=MESH_IDS)
    pl.semaphore_wait(barrier, groups - 1)
    mine = pl.ds(pl.multiple_of(me * width, 128), width)
    copies = []
    for step in range(1, groups):
        peer = lax.rem(me + step, groups)
        for part, dst in enumerate((x_ref, dy_ref)):
            copy = pltpu.make_async_remote_copy(
                src_ref=src_ref.at[:, pl.ds(part * width, width)],
                dst_ref=dst.at[:, mine],
                send_sem=send_sem.at[step, part],
                recv_sem=recv_sem.at[step, part],
                device_id=(home, peer),
                device_id_type=MESH_IDS,
            )
            copy.start()
            copies.append(copy)
    for part, dst in enumerate((x_ref, dy_ref)):
        local = pltpu.make_async_copy(
            src_ref.at[:, pl.ds(part * width, width)], dst.at[:, mine], local_sem.at[part]
        )
        local.start()
        copies.append(local)
    for copy in copies:
        copy.wait()


def dp_gather(chunk, groups, width):
    rows = chunk.shape[0]
    full = jax.ShapeDtypeStruct((rows, groups * width), chunk.dtype)
    return pl.pallas_call(
        lambda *refs: dp_gather_kernel(groups, width, *refs),
        out_shape=(full, full),
        in_specs=[pl.BlockSpec(memory_space=pl.ANY)],
        out_specs=(pl.BlockSpec(memory_space=pl.ANY), pl.BlockSpec(memory_space=pl.ANY)),
        scratch_shapes=[
            pltpu.SemaphoreType.DMA((2,)),
            pltpu.SemaphoreType.DMA((groups, 2)),
            pltpu.SemaphoreType.DMA((groups, 2)),
        ],
        compiler_params=pltpu.CompilerParams(collective_id=2, has_side_effects=True),
    )(chunk)


def from_behind(value, axis, by):
    devices = lax.axis_size(axis)
    return lax.ppermute(value, axis, [(i, (i + by) % devices) for i in range(devices)])


def pair_lookup(experts, pair_flags, half_axis):
    match = experts[:, None] % half_axis == jnp.arange(half_axis, dtype=jnp.int32)[None, :]
    return jnp.sum(jnp.where(match, pair_flags[None, :], 0), axis=1)


def shards(tokens, cotangent, gate_weight, up_weight, down_weight, expert_ids, gates, swap_flags):
    expert_count = lax.axis_size("expert")
    half_axis = expert_count // 2
    my_slot = lax.axis_index("expert")
    row_count, model_width = tokens.shape
    routed = expert_ids.shape[1]
    capacity = row_count * routed * 5 // (4 * expert_count)
    groups = lax.axis_size("dp")
    quarter = model_width // groups
    own_flag = pair_lookup(jnp.reshape(my_slot, (1,)), swap_flags, half_axis)[0]
    flat_ids = expert_ids.reshape(-1)
    weights = (gate_weight, up_weight, down_weight)
    arrived = from_behind((gate_weight, up_weight, down_weight), "expert", half_axis)
    weights = tuple(
        (jnp.where(own_flag == 1, fresh, stay) for fresh, stay in zip(arrived, weights))
    )
    flipped = pair_lookup(flat_ids, swap_flags, half_axis)
    target = jnp.where(flipped == 1, (flat_ids + half_axis) % expert_count, flat_ids)
    copies = row_count * routed
    onehot = (target[:, None] == jnp.arange(expert_count, dtype=jnp.int32)[None, :]).astype(
        jnp.int32
    )
    earlier = jnp.cumsum(onehot, axis=0) - onehot
    position = jnp.sum(earlier * onehot, axis=1)
    buffer_index = target * capacity + position
    source = jnp.zeros((expert_count * capacity,), jnp.int32)
    source = source.at[buffer_index].set(jnp.arange(copies, dtype=jnp.int32) + 1)
    filled = source > 0
    copy_index = jnp.maximum(source - 1, 0)
    token_index = copy_index // routed
    my_group = lax.axis_index("dp")
    x_part = lax.dynamic_slice_in_dim(tokens, my_group * quarter, quarter, axis=1)
    dy_part = lax.dynamic_slice_in_dim(cotangent, my_group * quarter, quarter, axis=1)
    x_buffer = jnp.where(filled[:, None], x_part[token_index], 0)
    dy_buffer = jnp.where(filled[:, None], dy_part[token_index], 0)
    gate_buffer = jnp.where(filled, gates.reshape(-1)[copy_index], 0)
    gate_cols = jnp.zeros((expert_count * capacity, 128), jnp.bfloat16).at[:, 0].set(gate_buffer)
    outgoing = jnp.concatenate([x_buffer, dy_buffer, gate_cols], axis=1)
    arrived = lax.all_to_all(outgoing, "expert", split_axis=0, concat_axis=0, tiled=True)
    x_rows, dy_rows = dp_gather(arrived, groups, quarter)
    gate_rows = arrived[:, 2 * quarter]
    w_gate = weights[0][0]
    w_up = weights[1][0]
    w_down = weights[2][0]
    contract_last = (((1,), (1,)), ((), ()))
    pre_gate = lax.dot_general(x_rows, w_gate, contract_last, preferred_element_type=jnp.float32)
    pre_up = lax.dot_general(x_rows, w_up, contract_last, preferred_element_type=jnp.float32)
    sigma = jax.nn.sigmoid(pre_gate)
    active = pre_gate * sigma
    hidden = (active * pre_up).astype(jnp.bfloat16)
    back = lax.dot_general(dy_rows, w_down, contract_last, preferred_element_type=jnp.float32)
    score_part = jnp.sum(hidden.astype(jnp.float32) * back, axis=1)
    grad_hidden = gate_rows.astype(jnp.float32)[:, None] * back
    slope = sigma * (1.0 + pre_gate * (1.0 - sigma))
    grad_gate = (grad_hidden * pre_up * slope).astype(jnp.bfloat16)
    grad_up = (grad_hidden * active).astype(jnp.bfloat16)
    input_part = jnp.dot(grad_gate, w_gate, preferred_element_type=jnp.float32)
    input_part = input_part + jnp.dot(grad_up, w_up, preferred_element_type=jnp.float32)
    scaled = gate_rows[:, None] * dy_rows
    contract_rows = (((0,), (0,)), ((), ()))
    grad_wgate = lax.dot_general(
        grad_gate, x_rows, contract_rows, preferred_element_type=jnp.float32
    )
    grad_wup = lax.dot_general(grad_up, x_rows, contract_rows, preferred_element_type=jnp.float32)
    grad_wdown = lax.dot_general(hidden, scaled, contract_rows, preferred_element_type=jnp.float32)
    score_cols = jnp.zeros((capacity * expert_count, 128), jnp.float32).at[:, 0].set(score_part)
    reduced = dp_scatter(input_part.astype(jnp.bfloat16), score_cols, groups)
    back_rows = lax.all_to_all(reduced, "expert", split_axis=0, concat_axis=0, tiled=True)
    per_copy = back_rows[buffer_index].reshape(row_count, routed, quarter + 128)
    input_grad = jnp.sum(per_copy[:, :, :quarter].astype(jnp.float32), axis=1).astype(jnp.bfloat16)
    gate_grad = per_copy[:, :, quarter]
    gradients = (
        grad_wgate.astype(jnp.bfloat16)[None],
        grad_wup.astype(jnp.bfloat16)[None],
        grad_wdown.astype(jnp.bfloat16)[None],
    )
    return (input_grad, gate_grad, gradients[0], gradients[1], gradients[2])


def solution(mesh):
    placed = (
        P("expert", None),
        P("expert", None),
        P("expert", "dp", None),
        P("expert", "dp", None),
        P("expert", "dp", None),
        P("expert", None),
        P("expert", None),
        P(),
    )
    return jax.shard_map(
        shards,
        mesh=mesh,
        in_specs=placed,
        out_specs=(
            P("expert", "dp"),
            P("expert", None),
            P("expert", "dp", None),
            P("expert", "dp", None),
            P("expert", "dp", None),
        ),
        check_vma=False,
    )
```

```python
import jax
import jax.numpy as jnp
from jax import lax
from jax.sharding import PartitionSpec as P
from jax.experimental import pallas as pl
from jax.experimental.pallas import tpu as pltpu

MESH_IDS = pl.DeviceIdType.MESH


def dp_scatter_kernel(groups, src_ref, score_ref, out_ref, score_out, landing, score_in, send_sem, recv_sem):
    me = lax.axis_index("dp")
    home = lax.axis_index("expert")
    width = landing.shape[2]
    barrier = pltpu.get_barrier_semaphore()
    for step in range(1, groups):
        peer = lax.rem(me + step, groups)
        pl.semaphore_signal(barrier, 1, device_id=(home, peer), device_id_type=MESH_IDS)
    pl.semaphore_wait(barrier, groups - 1)
    copies = []
    for step in range(1, groups):
        peer = lax.rem(me + step, groups)
        for part, (source, target) in enumerate(
            ((src_ref.at[:, pl.ds(pl.multiple_of(peer * width, 128), width)], landing), (score_ref, score_in))
        ):
            copy = pltpu.make_async_remote_copy(
                src_ref=source,
                dst_ref=target.at[step],
                send_sem=send_sem.at[step, part],
                recv_sem=recv_sem.at[step, part],
                device_id=(home, peer),
                device_id_type=MESH_IDS,
            )
            copy.start()
            copies.append(copy)
    for copy in copies:
        copy.wait()
    own = pl.multiple_of(me * width, 128)
    block = 64

    def body(i, carry):
        rows = pl.ds(pl.multiple_of(i * block, block), block)
        total = src_ref[rows, pl.ds(own, width)].astype(jnp.float32)
        for step in range(1, groups):
            total = total + landing[step, rows, :].astype(jnp.float32)
        out_ref[rows, :] = total.astype(out_ref.dtype)
        return carry

    lax.fori_loop(0, out_ref.shape[0] // block, body, 0)
    score = score_ref[...]
    for step in range(1, groups):
        score = score + score_in[step]
    score_out[...] = score


def dp_scatter(partial, score, groups):
    rows, full = partial.shape
    width = full // groups
    return pl.pallas_call(
        lambda *refs: dp_scatter_kernel(groups, *refs),
        out_shape=(
            jax.ShapeDtypeStruct((rows, width), partial.dtype),
            jax.ShapeDtypeStruct(score.shape, score.dtype),
        ),
        in_specs=[pl.BlockSpec(memory_space=pltpu.VMEM)] * 2,
        out_specs=(pl.BlockSpec(memory_space=pltpu.VMEM), pl.BlockSpec(memory_space=pltpu.VMEM)),
        scratch_shapes=[
            pltpu.VMEM((groups, rows, width), partial.dtype),
            pltpu.VMEM((groups,) + score.shape, score.dtype),
            pltpu.SemaphoreType.DMA((groups, 2)),
            pltpu.SemaphoreType.DMA((groups, 2)),
        ],
        compiler_params=pltpu.CompilerParams(collective_id=0, has_side_effects=True),
    )(partial, score)


def dp_gather_kernel(groups, width, src_ref, x_ref, dy_ref, local_sem, send_sem, recv_sem):
    me = lax.axis_index("dp")
    home = lax.axis_index("expert")
    barrier = pltpu.get_barrier_semaphore()
    for step in range(1, groups):
        peer = lax.rem(me + step, groups)
        pl.semaphore_signal(barrier, 1, device_id=(home, peer), device_id_type=MESH_IDS)
    pl.semaphore_wait(barrier, groups - 1)
    mine = pl.ds(pl.multiple_of(me * width, 128), width)
    copies = []
    for step in range(1, groups):
        peer = lax.rem(me + step, groups)
        for part, dst in enumerate((x_ref, dy_ref)):
            copy = pltpu.make_async_remote_copy(
                src_ref=src_ref.at[:, pl.ds(part * width, width)],
                dst_ref=dst.at[:, mine],
                send_sem=send_sem.at[step, part],
                recv_sem=recv_sem.at[step, part],
                device_id=(home, peer),
                device_id_type=MESH_IDS,
            )
            copy.start()
            copies.append(copy)
    for part, dst in enumerate((x_ref, dy_ref)):
        local = pltpu.make_async_copy(
            src_ref.at[:, pl.ds(part * width, width)], dst.at[:, mine], local_sem.at[part]
        )
        local.start()
        copies.append(local)
    for copy in copies:
        copy.wait()


def dp_gather(chunk, groups, width):
    rows = chunk.shape[0]
    full = jax.ShapeDtypeStruct((rows, groups * width), chunk.dtype)
    return pl.pallas_call(
        lambda *refs: dp_gather_kernel(groups, width, *refs),
        out_shape=(full, full),
        in_specs=[pl.BlockSpec(memory_space=pl.ANY)],
        out_specs=(pl.BlockSpec(memory_space=pl.ANY), pl.BlockSpec(memory_space=pl.ANY)),
        scratch_shapes=[
            pltpu.SemaphoreType.DMA((2,)),
            pltpu.SemaphoreType.DMA((groups, 2)),
            pltpu.SemaphoreType.DMA((groups, 2)),
        ],
        compiler_params=pltpu.CompilerParams(collective_id=2, has_side_effects=True),
    )(chunk)


def from_behind(value, axis, by):
    devices = lax.axis_size(axis)
    return lax.ppermute(value, axis, [(i, (i + by) % devices) for i in range(devices)])


def pair_lookup(experts, pair_flags, half_axis):
    match = experts[:, None] % half_axis == jnp.arange(half_axis, dtype=jnp.int32)[None, :]
    return jnp.sum(jnp.where(match, pair_flags[None, :], 0), axis=1)


def shards(tokens, cotangent, gate_weight, up_weight, down_weight, expert_ids, gates, swap_flags):
    expert_count = lax.axis_size("expert")
    half_axis = expert_count // 2
    my_slot = lax.axis_index("expert")
    row_count, model_width = tokens.shape
    routed = expert_ids.shape[1]
    capacity = row_count * routed * 5 // (4 * expert_count)
    groups = lax.axis_size("dp")
    quarter = model_width // groups
    own_flag = pair_lookup(jnp.reshape(my_slot, (1,)), swap_flags, half_axis)[0]
    flat_ids = expert_ids.reshape(-1)
    weights = (gate_weight, up_weight, down_weight)
    arrived = from_behind((gate_weight, up_weight, down_weight), "expert", half_axis)
    weights = tuple(
        (jnp.where(own_flag == 1, fresh, stay) for fresh, stay in zip(arrived, weights))
    )
    flipped = pair_lookup(flat_ids, swap_flags, half_axis)
    target = jnp.where(flipped == 1, (flat_ids + half_axis) % expert_count, flat_ids)
    copies = row_count * routed
    onehot = (target[:, None] == jnp.arange(expert_count, dtype=jnp.int32)[None, :]).astype(
        jnp.int32
    )
    earlier = jnp.cumsum(onehot, axis=0) - onehot
    position = jnp.sum(earlier * onehot, axis=1)
    buffer_index = target * capacity + position
    source = jnp.zeros((expert_count * capacity,), jnp.int32)
    source = source.at[buffer_index].set(jnp.arange(copies, dtype=jnp.int32) + 1)
    filled = source > 0
    copy_index = jnp.maximum(source - 1, 0)
    token_index = copy_index // routed
    my_group = lax.axis_index("dp")
    x_part = lax.dynamic_slice_in_dim(tokens, my_group * quarter, quarter, axis=1)
    dy_part = lax.dynamic_slice_in_dim(cotangent, my_group * quarter, quarter, axis=1)
    x_buffer = jnp.where(filled[:, None], x_part[token_index], 0)
    dy_buffer = jnp.where(filled[:, None], dy_part[token_index], 0)
    gate_buffer = jnp.where(filled, gates.reshape(-1)[copy_index], 0)
    gate_cols = jnp.zeros((expert_count * capacity, 128), jnp.bfloat16).at[:, 0].set(gate_buffer)
    outgoing = jnp.concatenate([x_buffer, dy_buffer, gate_cols], axis=1)
    arrived = lax.all_to_all(outgoing, "expert", split_axis=0, concat_axis=0, tiled=True)
    x_rows, dy_rows = dp_gather(arrived, groups, quarter)
    gate_rows = arrived[:, 2 * quarter]
    w_gate = weights[0][0]
    w_up = weights[1][0]
    w_down = weights[2][0]
    contract_last = (((1,), (1,)), ((), ()))
    pre_gate = lax.dot_general(x_rows, w_gate, contract_last, preferred_element_type=jnp.float32)
    pre_up = lax.dot_general(x_rows, w_up, contract_last, preferred_element_type=jnp.float32)
    sigma = jax.nn.sigmoid(pre_gate)
    active = pre_gate * sigma
    hidden = (active * pre_up).astype(jnp.bfloat16)
    back = lax.dot_general(dy_rows, w_down, contract_last, preferred_element_type=jnp.float32)
    score_part = jnp.sum(hidden.astype(jnp.float32) * back, axis=1)
    grad_hidden = gate_rows.astype(jnp.float32)[:, None] * back
    slope = sigma * (1.0 + pre_gate * (1.0 - sigma))
    grad_gate = (grad_hidden * pre_up * slope).astype(jnp.bfloat16)
    grad_up = (grad_hidden * active).astype(jnp.bfloat16)
    input_part = jnp.dot(grad_gate, w_gate, preferred_element_type=jnp.float32)
    input_part = input_part + jnp.dot(grad_up, w_up, preferred_element_type=jnp.float32)
    scaled = gate_rows[:, None] * dy_rows
    contract_rows = (((0,), (0,)), ((), ()))
    grad_wgate = lax.dot_general(
        grad_gate, x_rows, contract_rows, preferred_element_type=jnp.float32
    )
    grad_wup = lax.dot_general(grad_up, x_rows, contract_rows, preferred_element_type=jnp.float32)
    grad_wdown = lax.dot_general(hidden, scaled, contract_rows, preferred_element_type=jnp.float32)
    slots = capacity * expert_count
    score_tile = jnp.zeros((8 * 128,), jnp.float32).at[:slots].set(score_part).reshape(8, 128)
    share, score_sum = dp_scatter(input_part.astype(jnp.bfloat16), score_tile, groups)
    score_col = jnp.zeros((slots, 128), jnp.bfloat16).at[:, 0].set(
        score_sum.reshape(-1)[:slots].astype(jnp.bfloat16)
    )
    reduced = jnp.concatenate([share, score_col], axis=1)
    back_rows = lax.all_to_all(reduced, "expert", split_axis=0, concat_axis=0, tiled=True)
    per_copy = back_rows[buffer_index].reshape(row_count, routed, quarter + 128)
    input_grad = jnp.sum(per_copy[:, :, :quarter].astype(jnp.float32), axis=1).astype(jnp.bfloat16)
    gate_grad = per_copy[:, :, quarter]
    gradients = (
        grad_wgate.astype(jnp.bfloat16)[None],
        grad_wup.astype(jnp.bfloat16)[None],
        grad_wdown.astype(jnp.bfloat16)[None],
    )
    return (input_grad, gate_grad, gradients[0], gradients[1], gradients[2])


def solution(mesh):
    placed = (
        P("expert", None),
        P("expert", None),
        P("expert", "dp", None),
        P("expert", "dp", None),
        P("expert", "dp", None),
        P("expert", None),
        P("expert", None),
        P(),
    )
    return jax.shard_map(
        shards,
        mesh=mesh,
        in_specs=placed,
        out_specs=(
            P("expert", "dp"),
            P("expert", None),
            P("expert", "dp", None),
            P("expert", "dp", None),
            P("expert", "dp", None),
        ),
        check_vma=False,
    )
```

```python
import jax
import jax.numpy as jnp
from jax import lax
from jax.sharding import PartitionSpec as P
from jax.experimental import pallas as pl
from jax.experimental.pallas import tpu as pltpu

MESH_IDS = pl.DeviceIdType.MESH


def dp_scatter_kernel(groups, src_ref, score_ref, out_ref, score_out, landing, score_in, send_sem, recv_sem):
    me = lax.axis_index("dp")
    home = lax.axis_index("expert")
    width = landing.shape[2]
    barrier = pltpu.get_barrier_semaphore()
    for step in range(1, groups):
        peer = lax.rem(me + step, groups)
        pl.semaphore_signal(barrier, 1, device_id=(home, peer), device_id_type=MESH_IDS)
    pl.semaphore_wait(barrier, groups - 1)
    copies = []
    for step in range(1, groups):
        peer = lax.rem(me + step, groups)
        for part, (source, target) in enumerate(
            ((src_ref.at[:, pl.ds(pl.multiple_of(peer * width, 128), width)], landing), (score_ref, score_in))
        ):
            copy = pltpu.make_async_remote_copy(
                src_ref=source,
                dst_ref=target.at[step],
                send_sem=send_sem.at[step, part],
                recv_sem=recv_sem.at[step, part],
                device_id=(home, peer),
                device_id_type=MESH_IDS,
            )
            copy.start()
            copies.append(copy)
    for copy in copies:
        copy.wait()
    own = pl.multiple_of(me * width, 128)
    block = 64

    def body(i, carry):
        rows = pl.ds(pl.multiple_of(i * block, block), block)
        total = src_ref[rows, pl.ds(own, width)].astype(jnp.float32)
        for step in range(1, groups):
            total = total + landing[step, rows, :].astype(jnp.float32)
        out_ref[rows, :] = total.astype(out_ref.dtype)
        return carry

    lax.fori_loop(0, out_ref.shape[0] // block, body, 0)
    score = score_ref[...]
    for step in range(1, groups):
        score = score + score_in[step]
    score_out[...] = score


def dp_scatter(partial, score, groups):
    rows, full = partial.shape
    width = full // groups
    return pl.pallas_call(
        lambda *refs: dp_scatter_kernel(groups, *refs),
        out_shape=(
            jax.ShapeDtypeStruct((rows, width), partial.dtype),
            jax.ShapeDtypeStruct(score.shape, score.dtype),
        ),
        in_specs=[pl.BlockSpec(memory_space=pltpu.VMEM)] * 2,
        out_specs=(pl.BlockSpec(memory_space=pltpu.VMEM), pl.BlockSpec(memory_space=pltpu.VMEM)),
        scratch_shapes=[
            pltpu.VMEM((groups, rows, width), partial.dtype),
            pltpu.VMEM((groups,) + score.shape, score.dtype),
            pltpu.SemaphoreType.DMA((groups, 2)),
            pltpu.SemaphoreType.DMA((groups, 2)),
        ],
        compiler_params=pltpu.CompilerParams(collective_id=0, has_side_effects=True),
    )(partial, score)


def dp_gather_kernel(groups, width, src_ref, x_ref, dy_ref, local_sem, send_sem, recv_sem):
    me = lax.axis_index("dp")
    home = lax.axis_index("expert")
    barrier = pltpu.get_barrier_semaphore()
    for step in range(1, groups):
        peer = lax.rem(me + step, groups)
        pl.semaphore_signal(barrier, 1, device_id=(home, peer), device_id_type=MESH_IDS)
    pl.semaphore_wait(barrier, groups - 1)
    mine = pl.ds(pl.multiple_of(me * width, 128), width)
    copies = []
    for step in range(1, groups):
        peer = lax.rem(me + step, groups)
        for part, dst in enumerate((x_ref, dy_ref)):
            copy = pltpu.make_async_remote_copy(
                src_ref=src_ref.at[:, pl.ds(part * width, width)],
                dst_ref=dst.at[:, mine],
                send_sem=send_sem.at[step, part],
                recv_sem=recv_sem.at[step, part],
                device_id=(home, peer),
                device_id_type=MESH_IDS,
            )
            copy.start()
            copies.append(copy)
    for part, dst in enumerate((x_ref, dy_ref)):
        local = pltpu.make_async_copy(
            src_ref.at[:, pl.ds(part * width, width)], dst.at[:, mine], local_sem.at[part]
        )
        local.start()
        copies.append(local)
    for copy in copies:
        copy.wait()


def dp_gather(chunk, groups, width):
    rows = chunk.shape[0]
    full = jax.ShapeDtypeStruct((rows, groups * width), chunk.dtype)
    return pl.pallas_call(
        lambda *refs: dp_gather_kernel(groups, width, *refs),
        out_shape=(full, full),
        in_specs=[pl.BlockSpec(memory_space=pl.ANY)],
        out_specs=(pl.BlockSpec(memory_space=pl.ANY), pl.BlockSpec(memory_space=pl.ANY)),
        scratch_shapes=[
            pltpu.SemaphoreType.DMA((2,)),
            pltpu.SemaphoreType.DMA((groups, 2)),
            pltpu.SemaphoreType.DMA((groups, 2)),
        ],
        compiler_params=pltpu.CompilerParams(collective_id=2, has_side_effects=True),
    )(chunk)


def from_behind(value, axis, by):
    devices = lax.axis_size(axis)
    return lax.ppermute(value, axis, [(i, (i + by) % devices) for i in range(devices)])


def pair_lookup(experts, pair_flags, half_axis):
    match = experts[:, None] % half_axis == jnp.arange(half_axis, dtype=jnp.int32)[None, :]
    return jnp.sum(jnp.where(match, pair_flags[None, :], 0), axis=1)


def shards(tokens, cotangent, gate_weight, up_weight, down_weight, expert_ids, gates, swap_flags):
    expert_count = lax.axis_size("expert")
    half_axis = expert_count // 2
    my_slot = lax.axis_index("expert")
    row_count, model_width = tokens.shape
    routed = expert_ids.shape[1]
    capacity = row_count * routed * 5 // (4 * expert_count)
    groups = lax.axis_size("dp")
    quarter = model_width // groups
    own_flag = pair_lookup(jnp.reshape(my_slot, (1,)), swap_flags, half_axis)[0]
    flat_ids = expert_ids.reshape(-1)
    target = flat_ids
    copies = row_count * routed
    onehot = (target[:, None] == jnp.arange(expert_count, dtype=jnp.int32)[None, :]).astype(
        jnp.int32
    )
    earlier = jnp.cumsum(onehot, axis=0) - onehot
    position = jnp.sum(earlier * onehot, axis=1)
    buffer_index = target * capacity + position
    source = jnp.zeros((expert_count * capacity,), jnp.int32)
    source = source.at[buffer_index].set(jnp.arange(copies, dtype=jnp.int32) + 1)
    filled = source > 0
    copy_index = jnp.maximum(source - 1, 0)
    token_index = copy_index // routed
    my_group = lax.axis_index("dp")
    x_part = lax.dynamic_slice_in_dim(tokens, my_group * quarter, quarter, axis=1)
    dy_part = lax.dynamic_slice_in_dim(cotangent, my_group * quarter, quarter, axis=1)
    x_buffer = jnp.where(filled[:, None], x_part[token_index], 0)
    dy_buffer = jnp.where(filled[:, None], dy_part[token_index], 0)
    gate_buffer = jnp.where(filled, gates.reshape(-1)[copy_index], 0)
    gate_cols = jnp.zeros((expert_count * capacity, 128), jnp.bfloat16).at[:, 0].set(gate_buffer)
    outgoing = jnp.concatenate([x_buffer, dy_buffer, gate_cols], axis=1)
    arrived = lax.all_to_all(outgoing, "expert", split_axis=0, concat_axis=0, tiled=True)
    x_rows, dy_rows = dp_gather(arrived, groups, quarter)
    gate_rows = arrived[:, 2 * quarter]
    w_gate = gate_weight[0]
    w_up = up_weight[0]
    w_down = down_weight[0]
    contract_last = (((1,), (1,)), ((), ()))
    pre_gate = lax.dot_general(x_rows, w_gate, contract_last, preferred_element_type=jnp.float32)
    pre_up = lax.dot_general(x_rows, w_up, contract_last, preferred_element_type=jnp.float32)
    sigma = jax.nn.sigmoid(pre_gate)
    active = pre_gate * sigma
    hidden = (active * pre_up).astype(jnp.bfloat16)
    back = lax.dot_general(dy_rows, w_down, contract_last, preferred_element_type=jnp.float32)
    score_part = jnp.sum(hidden.astype(jnp.float32) * back, axis=1)
    grad_hidden = gate_rows.astype(jnp.float32)[:, None] * back
    slope = sigma * (1.0 + pre_gate * (1.0 - sigma))
    grad_gate = (grad_hidden * pre_up * slope).astype(jnp.bfloat16)
    grad_up = (grad_hidden * active).astype(jnp.bfloat16)
    input_part = jnp.dot(grad_gate, w_gate, preferred_element_type=jnp.float32)
    input_part = input_part + jnp.dot(grad_up, w_up, preferred_element_type=jnp.float32)
    scaled = gate_rows[:, None] * dy_rows
    contract_rows = (((0,), (0,)), ((), ()))
    grad_wgate = lax.dot_general(
        grad_gate, x_rows, contract_rows, preferred_element_type=jnp.float32
    )
    grad_wup = lax.dot_general(grad_up, x_rows, contract_rows, preferred_element_type=jnp.float32)
    grad_wdown = lax.dot_general(hidden, scaled, contract_rows, preferred_element_type=jnp.float32)
    local_grads = (
        grad_wgate.astype(jnp.bfloat16)[None],
        grad_wup.astype(jnp.bfloat16)[None],
        grad_wdown.astype(jnp.bfloat16)[None],
    )
    local_grads, input_part, score_part = lax.optimization_barrier(
        (local_grads, input_part, score_part)
    )
    arrived = from_behind(local_grads, "expert", half_axis)
    slots = capacity * expert_count
    score_tile = jnp.zeros((8 * 128,), jnp.float32).at[:slots].set(score_part).reshape(8, 128)
    share, score_sum = dp_scatter(input_part.astype(jnp.bfloat16), score_tile, groups)
    score_col = jnp.zeros((slots, 128), jnp.bfloat16).at[:, 0].set(
        score_sum.reshape(-1)[:slots].astype(jnp.bfloat16)
    )
    reduced = jnp.concatenate([share, score_col], axis=1)
    back_rows = lax.all_to_all(reduced, "expert", split_axis=0, concat_axis=0, tiled=True)
    per_copy = back_rows[buffer_index].reshape(row_count, routed, quarter + 128)
    input_grad = jnp.sum(per_copy[:, :, :quarter].astype(jnp.float32), axis=1).astype(jnp.bfloat16)
    gate_grad = per_copy[:, :, quarter]
    gradients = tuple(
        jnp.where(own_flag == 1, fresh, stay) for fresh, stay in zip(arrived, local_grads)
    )
    return (input_grad, gate_grad, gradients[0], gradients[1], gradients[2])


def solution(mesh):
    placed = (
        P("expert", None),
        P("expert", None),
        P("expert", "dp", None),
        P("expert", "dp", None),
        P("expert", "dp", None),
        P("expert", None),
        P("expert", None),
        P(),
    )
    return jax.shard_map(
        shards,
        mesh=mesh,
        in_specs=placed,
        out_specs=(
            P("expert", "dp"),
            P("expert", None),
            P("expert", "dp", None),
            P("expert", "dp", None),
            P("expert", "dp", None),
        ),
        check_vma=False,
    )
```

```python
import jax
import jax.numpy as jnp
from jax import lax
from jax.sharding import PartitionSpec as P
from jax.experimental import pallas as pl
from jax.experimental.pallas import tpu as pltpu

MESH_IDS = pl.DeviceIdType.MESH


def dp_scatter_kernel(groups, src_ref, score_ref, out_ref, score_out, landing, score_in, send_sem, recv_sem):
    me = lax.axis_index("dp")
    home = lax.axis_index("expert")
    width = landing.shape[2]
    barrier = pltpu.get_barrier_semaphore()
    for step in range(1, groups):
        peer = lax.rem(me + step, groups)
        pl.semaphore_signal(barrier, 1, device_id=(home, peer), device_id_type=MESH_IDS)
    pl.semaphore_wait(barrier, groups - 1)
    copies = []
    for step in range(1, groups):
        peer = lax.rem(me + step, groups)
        for part, (source, target) in enumerate(
            ((src_ref.at[:, pl.ds(pl.multiple_of(peer * width, 128), width)], landing), (score_ref, score_in))
        ):
            copy = pltpu.make_async_remote_copy(
                src_ref=source,
                dst_ref=target.at[step],
                send_sem=send_sem.at[step, part],
                recv_sem=recv_sem.at[step, part],
                device_id=(home, peer),
                device_id_type=MESH_IDS,
            )
            copy.start()
            copies.append(copy)
    for copy in copies:
        copy.wait()
    own = pl.multiple_of(me * width, 128)
    block = 64

    def body(i, carry):
        rows = pl.ds(pl.multiple_of(i * block, block), block)
        total = src_ref[rows, pl.ds(own, width)].astype(jnp.float32)
        for step in range(1, groups):
            total = total + landing[step, rows, :].astype(jnp.float32)
        out_ref[rows, :] = total.astype(out_ref.dtype)
        return carry

    lax.fori_loop(0, out_ref.shape[0] // block, body, 0)
    score = score_ref[...]
    for step in range(1, groups):
        score = score + score_in[step]
    score_out[...] = score


def dp_scatter(partial, score, groups):
    rows, full = partial.shape
    width = full // groups
    return pl.pallas_call(
        lambda *refs: dp_scatter_kernel(groups, *refs),
        out_shape=(
            jax.ShapeDtypeStruct((rows, width), partial.dtype),
            jax.ShapeDtypeStruct(score.shape, score.dtype),
        ),
        in_specs=[pl.BlockSpec(memory_space=pltpu.VMEM)] * 2,
        out_specs=(pl.BlockSpec(memory_space=pltpu.VMEM), pl.BlockSpec(memory_space=pltpu.VMEM)),
        scratch_shapes=[
            pltpu.VMEM((groups, rows, width), partial.dtype),
            pltpu.VMEM((groups,) + score.shape, score.dtype),
            pltpu.SemaphoreType.DMA((groups, 2)),
            pltpu.SemaphoreType.DMA((groups, 2)),
        ],
        compiler_params=pltpu.CompilerParams(collective_id=0, has_side_effects=True),
    )(partial, score)


def pair_swap_kernel(width, src_ref, x_ref, dy_ref, local_sem, send_sem, recv_sem):
    me = lax.axis_index("dp")
    home = lax.axis_index("expert")
    side = lax.rem(me, 2)
    partner = me + 1 - 2 * side
    barrier = pltpu.get_barrier_semaphore()
    pl.semaphore_signal(barrier, 1, device_id=(home, partner), device_id_type=MESH_IDS)
    pl.semaphore_wait(barrier, 1)
    mine = pl.ds(pl.multiple_of(side * width, 128), width)
    copies = []
    for part, dst in enumerate((x_ref, dy_ref)):
        copy = pltpu.make_async_remote_copy(
            src_ref=src_ref.at[:, pl.ds(part * width, width)],
            dst_ref=dst.at[:, mine],
            send_sem=send_sem.at[part],
            recv_sem=recv_sem.at[part],
            device_id=(home, partner),
            device_id_type=MESH_IDS,
        )
        copy.start()
        copies.append(copy)
    for part, dst in enumerate((x_ref, dy_ref)):
        local = pltpu.make_async_copy(
            src_ref.at[:, pl.ds(part * width, width)], dst.at[:, mine], local_sem.at[part]
        )
        local.start()
        copies.append(local)
    for copy in copies:
        copy.wait()


def pair_swap(chunk, width):
    rows = chunk.shape[0]
    full = jax.ShapeDtypeStruct((rows, 2 * width), chunk.dtype)
    return pl.pallas_call(
        lambda *refs: pair_swap_kernel(width, *refs),
        out_shape=(full, full),
        in_specs=[pl.BlockSpec(memory_space=pl.ANY)],
        out_specs=(pl.BlockSpec(memory_space=pl.ANY), pl.BlockSpec(memory_space=pl.ANY)),
        scratch_shapes=[
            pltpu.SemaphoreType.DMA((2,)),
            pltpu.SemaphoreType.DMA((2,)),
            pltpu.SemaphoreType.DMA((2,)),
        ],
        compiler_params=pltpu.CompilerParams(collective_id=2, has_side_effects=True),
    )(chunk)


def from_behind(value, axis, by):
    devices = lax.axis_size(axis)
    return lax.ppermute(value, axis, [(i, (i + by) % devices) for i in range(devices)])


def pair_lookup(experts, pair_flags, half_axis):
    match = experts[:, None] % half_axis == jnp.arange(half_axis, dtype=jnp.int32)[None, :]
    return jnp.sum(jnp.where(match, pair_flags[None, :], 0), axis=1)


def shards(tokens, cotangent, gate_weight, up_weight, down_weight, expert_ids, gates, swap_flags):
    expert_count = lax.axis_size("expert")
    half_axis = expert_count // 2
    my_slot = lax.axis_index("expert")
    row_count, model_width = tokens.shape
    routed = expert_ids.shape[1]
    capacity = row_count * routed * 5 // (4 * expert_count)
    groups = lax.axis_size("dp")
    quarter = model_width // groups
    own_flag = pair_lookup(jnp.reshape(my_slot, (1,)), swap_flags, half_axis)[0]
    flat_ids = expert_ids.reshape(-1)
    weights = (gate_weight, up_weight, down_weight)
    arrived = from_behind((gate_weight, up_weight, down_weight), "expert", half_axis)
    weights = tuple(
        (jnp.where(own_flag == 1, fresh, stay) for fresh, stay in zip(arrived, weights))
    )
    flipped = pair_lookup(flat_ids, swap_flags, half_axis)
    target = jnp.where(flipped == 1, (flat_ids + half_axis) % expert_count, flat_ids)
    copies = row_count * routed
    onehot = (target[:, None] == jnp.arange(expert_count, dtype=jnp.int32)[None, :]).astype(
        jnp.int32
    )
    earlier = jnp.cumsum(onehot, axis=0) - onehot
    position = jnp.sum(earlier * onehot, axis=1)
    buffer_index = target * capacity + position
    source = jnp.zeros((expert_count * capacity,), jnp.int32)
    source = source.at[buffer_index].set(jnp.arange(copies, dtype=jnp.int32) + 1)
    filled = source > 0
    copy_index = jnp.maximum(source - 1, 0)
    token_index = copy_index // routed
    half = model_width // 2
    my_side = lax.rem(lax.axis_index("dp"), 2)
    x_part = lax.dynamic_slice_in_dim(tokens, my_side * half, half, axis=1)
    dy_part = lax.dynamic_slice_in_dim(cotangent, my_side * half, half, axis=1)
    x_buffer = jnp.where(filled[:, None], x_part[token_index], 0)
    dy_buffer = jnp.where(filled[:, None], dy_part[token_index], 0)
    gate_buffer = jnp.where(filled, gates.reshape(-1)[copy_index], 0)
    gate_cols = jnp.zeros((expert_count * capacity, 128), jnp.bfloat16).at[:, 0].set(gate_buffer)
    outgoing = jnp.concatenate([x_buffer, dy_buffer, gate_cols], axis=1)
    arrived = lax.all_to_all(outgoing, "expert", split_axis=0, concat_axis=0, tiled=True)
    x_rows, dy_rows = pair_swap(arrived, half)
    gate_rows = arrived[:, 2 * half]
    w_gate = weights[0][0]
    w_up = weights[1][0]
    w_down = weights[2][0]
    contract_last = (((1,), (1,)), ((), ()))
    pre_gate = lax.dot_general(x_rows, w_gate, contract_last, preferred_element_type=jnp.float32)
    pre_up = lax.dot_general(x_rows, w_up, contract_last, preferred_element_type=jnp.float32)
    sigma = jax.nn.sigmoid(pre_gate)
    active = pre_gate * sigma
    hidden = (active * pre_up).astype(jnp.bfloat16)
    back = lax.dot_general(dy_rows, w_down, contract_last, preferred_element_type=jnp.float32)
    score_part = jnp.sum(hidden.astype(jnp.float32) * back, axis=1)
    grad_hidden = gate_rows.astype(jnp.float32)[:, None] * back
    slope = sigma * (1.0 + pre_gate * (1.0 - sigma))
    grad_gate = (grad_hidden * pre_up * slope).astype(jnp.bfloat16)
    grad_up = (grad_hidden * active).astype(jnp.bfloat16)
    input_part = jnp.dot(grad_gate, w_gate, preferred_element_type=jnp.float32)
    input_part = input_part + jnp.dot(grad_up, w_up, preferred_element_type=jnp.float32)
    scaled = gate_rows[:, None] * dy_rows
    contract_rows = (((0,), (0,)), ((), ()))
    grad_wgate = lax.dot_general(
        grad_gate, x_rows, contract_rows, preferred_element_type=jnp.float32
    )
    grad_wup = lax.dot_general(grad_up, x_rows, contract_rows, preferred_element_type=jnp.float32)
    grad_wdown = lax.dot_general(hidden, scaled, contract_rows, preferred_element_type=jnp.float32)
    slots = capacity * expert_count
    score_tile = jnp.zeros((8 * 128,), jnp.float32).at[:slots].set(score_part).reshape(8, 128)
    share, score_sum = dp_scatter(input_part.astype(jnp.bfloat16), score_tile, groups)
    score_col = jnp.zeros((slots, 128), jnp.bfloat16).at[:, 0].set(
        score_sum.reshape(-1)[:slots].astype(jnp.bfloat16)
    )
    reduced = jnp.concatenate([share, score_col], axis=1)
    back_rows = lax.all_to_all(reduced, "expert", split_axis=0, concat_axis=0, tiled=True)
    per_copy = back_rows[buffer_index].reshape(row_count, routed, quarter + 128)
    input_grad = jnp.sum(per_copy[:, :, :quarter].astype(jnp.float32), axis=1).astype(jnp.bfloat16)
    gate_grad = per_copy[:, :, quarter]
    gradients = (
        grad_wgate.astype(jnp.bfloat16)[None],
        grad_wup.astype(jnp.bfloat16)[None],
        grad_wdown.astype(jnp.bfloat16)[None],
    )
    return (input_grad, gate_grad, gradients[0], gradients[1], gradients[2])


def solution(mesh):
    placed = (
        P("expert", None),
        P("expert", None),
        P("expert", "dp", None),
        P("expert", "dp", None),
        P("expert", "dp", None),
        P("expert", None),
        P("expert", None),
        P(),
    )
    return jax.shard_map(
        shards,
        mesh=mesh,
        in_specs=placed,
        out_specs=(
            P("expert", "dp"),
            P("expert", None),
            P("expert", "dp", None),
            P("expert", "dp", None),
            P("expert", "dp", None),
        ),
        check_vma=False,
    )
```

```python
import jax
import jax.numpy as jnp
from jax import lax
from jax.sharding import PartitionSpec as P
from jax.experimental import pallas as pl
from jax.experimental.pallas import tpu as pltpu

MESH_IDS = pl.DeviceIdType.MESH


def dp_scatter_kernel(groups, src_ref, score_ref, out_ref, score_out, landing, score_in, send_sem, recv_sem):
    me = lax.axis_index("dp")
    home = lax.axis_index("expert")
    width = landing.shape[2]
    barrier = pltpu.get_barrier_semaphore()
    for step in range(1, groups):
        peer = lax.rem(me + step, groups)
        pl.semaphore_signal(barrier, 1, device_id=(home, peer), device_id_type=MESH_IDS)
    pl.semaphore_wait(barrier, groups - 1)
    copies = []
    for step in range(1, groups):
        peer = lax.rem(me + step, groups)
        for part, (source, target) in enumerate(
            ((src_ref.at[:, pl.ds(pl.multiple_of(peer * width, 128), width)], landing), (score_ref, score_in))
        ):
            copy = pltpu.make_async_remote_copy(
                src_ref=source,
                dst_ref=target.at[step],
                send_sem=send_sem.at[step, part],
                recv_sem=recv_sem.at[step, part],
                device_id=(home, peer),
                device_id_type=MESH_IDS,
            )
            copy.start()
            copies.append(copy)
    for copy in copies:
        copy.wait()
    own = pl.multiple_of(me * width, 128)
    block = 64

    def body(i, carry):
        rows = pl.ds(pl.multiple_of(i * block, block), block)
        total = src_ref[rows, pl.ds(own, width)].astype(jnp.float32)
        for step in range(1, groups):
            total = total + landing[step, rows, :].astype(jnp.float32)
        out_ref[rows, :] = total.astype(out_ref.dtype)
        return carry

    lax.fori_loop(0, out_ref.shape[0] // block, body, 0)
    score = score_ref[...]
    for step in range(1, groups):
        score = score + score_in[step]
    score_out[...] = score


def dp_scatter(partial, score, groups):
    rows, full = partial.shape
    width = full // groups
    return pl.pallas_call(
        lambda *refs: dp_scatter_kernel(groups, *refs),
        out_shape=(
            jax.ShapeDtypeStruct((rows, width), partial.dtype),
            jax.ShapeDtypeStruct(score.shape, score.dtype),
        ),
        in_specs=[pl.BlockSpec(memory_space=pltpu.VMEM)] * 2,
        out_specs=(pl.BlockSpec(memory_space=pltpu.VMEM), pl.BlockSpec(memory_space=pltpu.VMEM)),
        scratch_shapes=[
            pltpu.VMEM((groups, rows, width), partial.dtype),
            pltpu.VMEM((groups,) + score.shape, score.dtype),
            pltpu.SemaphoreType.DMA((groups, 2)),
            pltpu.SemaphoreType.DMA((groups, 2)),
        ],
        compiler_params=pltpu.CompilerParams(collective_id=0, has_side_effects=True),
    )(partial, score)


def dp_gather_kernel(groups, width, src_ref, x_ref, dy_ref, local_sem, send_sem, recv_sem):
    me = lax.axis_index("dp")
    home = lax.axis_index("expert")
    barrier = pltpu.get_barrier_semaphore()
    for step in range(1, groups):
        peer = lax.rem(me + step, groups)
        pl.semaphore_signal(barrier, 1, device_id=(home, peer), device_id_type=MESH_IDS)
    pl.semaphore_wait(barrier, groups - 1)
    mine = pl.ds(pl.multiple_of(me * width, 128), width)
    copies = []
    for step in range(1, groups):
        peer = lax.rem(me + step, groups)
        for part, dst in enumerate((x_ref, dy_ref)):
            copy = pltpu.make_async_remote_copy(
                src_ref=src_ref.at[:, pl.ds(part * width, width)],
                dst_ref=dst.at[:, mine],
                send_sem=send_sem.at[step, part],
                recv_sem=recv_sem.at[step, part],
                device_id=(home, peer),
                device_id_type=MESH_IDS,
            )
            copy.start()
            copies.append(copy)
    for part, dst in enumerate((x_ref, dy_ref)):
        local = pltpu.make_async_copy(
            src_ref.at[:, pl.ds(part * width, width)], dst.at[:, mine], local_sem.at[part]
        )
        local.start()
        copies.append(local)
    for copy in copies:
        copy.wait()


def dp_gather(chunk, groups, width):
    rows = chunk.shape[0]
    full = jax.ShapeDtypeStruct((rows, groups * width), chunk.dtype)
    return pl.pallas_call(
        lambda *refs: dp_gather_kernel(groups, width, *refs),
        out_shape=(full, full),
        in_specs=[pl.BlockSpec(memory_space=pl.ANY)],
        out_specs=(pl.BlockSpec(memory_space=pl.ANY), pl.BlockSpec(memory_space=pl.ANY)),
        scratch_shapes=[
            pltpu.SemaphoreType.DMA((2,)),
            pltpu.SemaphoreType.DMA((groups, 2)),
            pltpu.SemaphoreType.DMA((groups, 2)),
        ],
        compiler_params=pltpu.CompilerParams(collective_id=2, has_side_effects=True),
    )(chunk)


def from_behind(value, axis, by):
    devices = lax.axis_size(axis)
    return lax.ppermute(value, axis, [(i, (i + by) % devices) for i in range(devices)])


def z_shift(value, expert_count, groups, delta):
    half_axis = expert_count // 2
    ring = 2 * groups
    pairs = []
    for slot in range(expert_count):
        for group in range(groups):
            z = (slot // half_axis) * groups + group
            moved = (z + delta) % ring
            target = (moved // groups) * half_axis + slot % half_axis
            pairs.append((slot * groups + group, target * groups + moved % groups))
    return lax.ppermute(value, ("expert", "dp"), pairs)


def across_z(value, expert_count, groups):
    split = value.shape[1] // 2
    ahead = value[:, :split]
    behind = value[:, split:]
    for _ in range(2):
        ahead = z_shift(ahead, expert_count, groups, 2)
        behind = z_shift(behind, expert_count, groups, -2)
    return jnp.concatenate([ahead, behind], axis=1)


def pair_lookup(experts, pair_flags, half_axis):
    match = experts[:, None] % half_axis == jnp.arange(half_axis, dtype=jnp.int32)[None, :]
    return jnp.sum(jnp.where(match, pair_flags[None, :], 0), axis=1)


def shards(tokens, cotangent, gate_weight, up_weight, down_weight, expert_ids, gates, swap_flags):
    expert_count = lax.axis_size("expert")
    half_axis = expert_count // 2
    my_slot = lax.axis_index("expert")
    row_count, model_width = tokens.shape
    routed = expert_ids.shape[1]
    capacity = row_count * routed * 5 // (4 * expert_count)
    groups = lax.axis_size("dp")
    quarter = model_width // groups
    own_flag = pair_lookup(jnp.reshape(my_slot, (1,)), swap_flags, half_axis)[0]
    flat_ids = expert_ids.reshape(-1)
    weights = (gate_weight, up_weight, down_weight)
    arrived = tuple(
        across_z(w, expert_count, groups) for w in (gate_weight, up_weight, down_weight)
    )
    weights = tuple(
        (jnp.where(own_flag == 1, fresh, stay) for fresh, stay in zip(arrived, weights))
    )
    flipped = pair_lookup(flat_ids, swap_flags, half_axis)
    target = jnp.where(flipped == 1, (flat_ids + half_axis) % expert_count, flat_ids)
    copies = row_count * routed
    onehot = (target[:, None] == jnp.arange(expert_count, dtype=jnp.int32)[None, :]).astype(
        jnp.int32
    )
    earlier = jnp.cumsum(onehot, axis=0) - onehot
    position = jnp.sum(earlier * onehot, axis=1)
    buffer_index = target * capacity + position
    source = jnp.zeros((expert_count * capacity,), jnp.int32)
    source = source.at[buffer_index].set(jnp.arange(copies, dtype=jnp.int32) + 1)
    filled = source > 0
    copy_index = jnp.maximum(source - 1, 0)
    token_index = copy_index // routed
    my_group = lax.axis_index("dp")
    x_part = lax.dynamic_slice_in_dim(tokens, my_group * quarter, quarter, axis=1)
    dy_part = lax.dynamic_slice_in_dim(cotangent, my_group * quarter, quarter, axis=1)
    x_buffer = jnp.where(filled[:, None], x_part[token_index], 0)
    dy_buffer = jnp.where(filled[:, None], dy_part[token_index], 0)
    gate_buffer = jnp.where(filled, gates.reshape(-1)[copy_index], 0)
    gate_cols = jnp.zeros((expert_count * capacity, 128), jnp.bfloat16).at[:, 0].set(gate_buffer)
    outgoing = jnp.concatenate([x_buffer, dy_buffer, gate_cols], axis=1)
    arrived = lax.all_to_all(outgoing, "expert", split_axis=0, concat_axis=0, tiled=True)
    x_rows, dy_rows = dp_gather(arrived, groups, quarter)
    gate_rows = arrived[:, 2 * quarter]
    w_gate = weights[0][0]
    w_up = weights[1][0]
    w_down = weights[2][0]
    contract_last = (((1,), (1,)), ((), ()))
    pre_gate = lax.dot_general(x_rows, w_gate, contract_last, preferred_element_type=jnp.float32)
    pre_up = lax.dot_general(x_rows, w_up, contract_last, preferred_element_type=jnp.float32)
    sigma = jax.nn.sigmoid(pre_gate)
    active = pre_gate * sigma
    hidden = (active * pre_up).astype(jnp.bfloat16)
    back = lax.dot_general(dy_rows, w_down, contract_last, preferred_element_type=jnp.float32)
    score_part = jnp.sum(hidden.astype(jnp.float32) * back, axis=1)
    grad_hidden = gate_rows.astype(jnp.float32)[:, None] * back
    slope = sigma * (1.0 + pre_gate * (1.0 - sigma))
    grad_gate = (grad_hidden * pre_up * slope).astype(jnp.bfloat16)
    grad_up = (grad_hidden * active).astype(jnp.bfloat16)
    input_part = jnp.dot(grad_gate, w_gate, preferred_element_type=jnp.float32)
    input_part = input_part + jnp.dot(grad_up, w_up, preferred_element_type=jnp.float32)
    scaled = gate_rows[:, None] * dy_rows
    contract_rows = (((0,), (0,)), ((), ()))
    grad_wgate = lax.dot_general(
        grad_gate, x_rows, contract_rows, preferred_element_type=jnp.float32
    )
    grad_wup = lax.dot_general(grad_up, x_rows, contract_rows, preferred_element_type=jnp.float32)
    grad_wdown = lax.dot_general(hidden, scaled, contract_rows, preferred_element_type=jnp.float32)
    slots = capacity * expert_count
    score_tile = jnp.zeros((8 * 128,), jnp.float32).at[:slots].set(score_part).reshape(8, 128)
    share, score_sum = dp_scatter(input_part.astype(jnp.bfloat16), score_tile, groups)
    score_col = jnp.zeros((slots, 128), jnp.bfloat16).at[:, 0].set(
        score_sum.reshape(-1)[:slots].astype(jnp.bfloat16)
    )
    reduced = jnp.concatenate([share, score_col], axis=1)
    back_rows = lax.all_to_all(reduced, "expert", split_axis=0, concat_axis=0, tiled=True)
    per_copy = back_rows[buffer_index].reshape(row_count, routed, quarter + 128)
    input_grad = jnp.sum(per_copy[:, :, :quarter].astype(jnp.float32), axis=1).astype(jnp.bfloat16)
    gate_grad = per_copy[:, :, quarter]
    gradients = (
        grad_wgate.astype(jnp.bfloat16)[None],
        grad_wup.astype(jnp.bfloat16)[None],
        grad_wdown.astype(jnp.bfloat16)[None],
    )
    return (input_grad, gate_grad, gradients[0], gradients[1], gradients[2])


def solution(mesh):
    placed = (
        P("expert", None),
        P("expert", None),
        P("expert", "dp", None),
        P("expert", "dp", None),
        P("expert", "dp", None),
        P("expert", None),
        P("expert", None),
        P(),
    )
    return jax.shard_map(
        shards,
        mesh=mesh,
        in_specs=placed,
        out_specs=(
            P("expert", "dp"),
            P("expert", None),
            P("expert", "dp", None),
            P("expert", "dp", None),
            P("expert", "dp", None),
        ),
        check_vma=False,
    )
```

```python
import jax
import jax.numpy as jnp
from jax import lax
from jax.sharding import PartitionSpec as P
from jax.experimental import pallas as pl
from jax.experimental.pallas import tpu as pltpu

MESH_IDS = pl.DeviceIdType.MESH


def dp_scatter_kernel(groups, src_ref, score_ref, out_ref, score_out, landing, score_in, send_sem, recv_sem):
    me = lax.axis_index("dp")
    home = lax.axis_index("expert")
    width = landing.shape[2]
    barrier = pltpu.get_barrier_semaphore()
    for step in range(1, groups):
        peer = lax.rem(me + step, groups)
        pl.semaphore_signal(barrier, 1, device_id=(home, peer), device_id_type=MESH_IDS)
    pl.semaphore_wait(barrier, groups - 1)
    copies = []
    for step in range(1, groups):
        peer = lax.rem(me + step, groups)
        for part, (source, target) in enumerate(
            ((src_ref.at[:, pl.ds(pl.multiple_of(peer * width, 128), width)], landing), (score_ref, score_in))
        ):
            copy = pltpu.make_async_remote_copy(
                src_ref=source,
                dst_ref=target.at[step],
                send_sem=send_sem.at[step, part],
                recv_sem=recv_sem.at[step, part],
                device_id=(home, peer),
                device_id_type=MESH_IDS,
            )
            copy.start()
            copies.append(copy)
    for copy in copies:
        copy.wait()
    own = pl.multiple_of(me * width, 128)
    block = 64

    def body(i, carry):
        rows = pl.ds(pl.multiple_of(i * block, block), block)
        total = src_ref[rows, pl.ds(own, width)].astype(jnp.float32)
        for step in range(1, groups):
            total = total + landing[step, rows, :].astype(jnp.float32)
        out_ref[rows, :] = total.astype(out_ref.dtype)
        return carry

    lax.fori_loop(0, out_ref.shape[0] // block, body, 0)
    score = score_ref[...]
    for step in range(1, groups):
        score = score + score_in[step]
    score_out[...] = score


def dp_scatter(partial, score, groups):
    rows, full = partial.shape
    width = full // groups
    return pl.pallas_call(
        lambda *refs: dp_scatter_kernel(groups, *refs),
        out_shape=(
            jax.ShapeDtypeStruct((rows, width), partial.dtype),
            jax.ShapeDtypeStruct(score.shape, score.dtype),
        ),
        in_specs=[pl.BlockSpec(memory_space=pltpu.VMEM)] * 2,
        out_specs=(pl.BlockSpec(memory_space=pltpu.VMEM), pl.BlockSpec(memory_space=pltpu.VMEM)),
        scratch_shapes=[
            pltpu.VMEM((groups, rows, width), partial.dtype),
            pltpu.VMEM((groups,) + score.shape, score.dtype),
            pltpu.SemaphoreType.DMA((groups, 2)),
            pltpu.SemaphoreType.DMA((groups, 2)),
        ],
        compiler_params=pltpu.CompilerParams(collective_id=0, has_side_effects=True),
    )(partial, score)


def dp_gather_kernel(groups, width, src_ref, x_ref, dy_ref, local_sem, send_sem, recv_sem):
    me = lax.axis_index("dp")
    home = lax.axis_index("expert")
    barrier = pltpu.get_barrier_semaphore()
    for step in range(1, groups):
        peer = lax.rem(me + step, groups)
        pl.semaphore_signal(barrier, 1, device_id=(home, peer), device_id_type=MESH_IDS)
    pl.semaphore_wait(barrier, groups - 1)
    mine = pl.ds(pl.multiple_of(me * width, 128), width)
    copies = []
    for step in range(1, groups):
        peer = lax.rem(me + step, groups)
        for part, dst in enumerate((x_ref, dy_ref)):
            copy = pltpu.make_async_remote_copy(
                src_ref=src_ref.at[:, pl.ds(part * width, width)],
                dst_ref=dst.at[:, mine],
                send_sem=send_sem.at[step, part],
                recv_sem=recv_sem.at[step, part],
                device_id=(home, peer),
                device_id_type=MESH_IDS,
            )
            copy.start()
            copies.append(copy)
    for part, dst in enumerate((x_ref, dy_ref)):
        local = pltpu.make_async_copy(
            src_ref.at[:, pl.ds(part * width, width)], dst.at[:, mine], local_sem.at[part]
        )
        local.start()
        copies.append(local)
    for copy in copies:
        copy.wait()


def dp_gather(chunk, groups, width):
    rows = chunk.shape[0]
    full = jax.ShapeDtypeStruct((rows, groups * width), chunk.dtype)
    return pl.pallas_call(
        lambda *refs: dp_gather_kernel(groups, width, *refs),
        out_shape=(full, full),
        in_specs=[pl.BlockSpec(memory_space=pl.ANY)],
        out_specs=(pl.BlockSpec(memory_space=pl.ANY), pl.BlockSpec(memory_space=pl.ANY)),
        scratch_shapes=[
            pltpu.SemaphoreType.DMA((2,)),
            pltpu.SemaphoreType.DMA((groups, 2)),
            pltpu.SemaphoreType.DMA((groups, 2)),
        ],
        compiler_params=pltpu.CompilerParams(collective_id=2, has_side_effects=True),
    )(chunk)


def from_behind(value, axis, by):
    devices = lax.axis_size(axis)
    return lax.ppermute(value, axis, [(i, (i + by) % devices) for i in range(devices)])


def z_shift(value, expert_count, groups, delta):
    half_axis = expert_count // 2
    ring = 2 * groups
    pairs = []
    for slot in range(expert_count):
        for group in range(groups):
            z = (slot // half_axis) * groups + group
            moved = (z + delta) % ring
            target = (moved // groups) * half_axis + slot % half_axis
            pairs.append((slot * groups + group, target * groups + moved % groups))
    return lax.ppermute(value, ("expert", "dp"), pairs)


def across_z(value, expert_count, groups, ready):
    split = value.shape[1] // 2
    ahead = z_shift(value[:, :split], expert_count, groups, 2)
    behind = z_shift(value[:, split:], expert_count, groups, -2)
    ahead, behind, ready = lax.optimization_barrier((ahead, behind, ready))
    ahead = z_shift(ahead, expert_count, groups, 2)
    behind = z_shift(behind, expert_count, groups, -2)
    return jnp.concatenate([ahead, behind], axis=1), ready

def pair_lookup(experts, pair_flags, half_axis):
    match = experts[:, None] % half_axis == jnp.arange(half_axis, dtype=jnp.int32)[None, :]
    return jnp.sum(jnp.where(match, pair_flags[None, :], 0), axis=1)


def shards(tokens, cotangent, gate_weight, up_weight, down_weight, expert_ids, gates, swap_flags):
    expert_count = lax.axis_size("expert")
    half_axis = expert_count // 2
    my_slot = lax.axis_index("expert")
    row_count, model_width = tokens.shape
    routed = expert_ids.shape[1]
    capacity = row_count * routed * 5 // (4 * expert_count)
    groups = lax.axis_size("dp")
    quarter = model_width // groups
    own_flag = pair_lookup(jnp.reshape(my_slot, (1,)), swap_flags, half_axis)[0]
    flat_ids = expert_ids.reshape(-1)
    weights = (gate_weight, up_weight, down_weight)
    flipped = pair_lookup(flat_ids, swap_flags, half_axis)
    target = jnp.where(flipped == 1, (flat_ids + half_axis) % expert_count, flat_ids)
    copies = row_count * routed
    onehot = (target[:, None] == jnp.arange(expert_count, dtype=jnp.int32)[None, :]).astype(
        jnp.int32
    )
    earlier = jnp.cumsum(onehot, axis=0) - onehot
    position = jnp.sum(earlier * onehot, axis=1)
    buffer_index = target * capacity + position
    source = jnp.zeros((expert_count * capacity,), jnp.int32)
    source = source.at[buffer_index].set(jnp.arange(copies, dtype=jnp.int32) + 1)
    filled = source > 0
    copy_index = jnp.maximum(source - 1, 0)
    token_index = copy_index // routed
    my_group = lax.axis_index("dp")
    x_part = lax.dynamic_slice_in_dim(tokens, my_group * quarter, quarter, axis=1)
    dy_part = lax.dynamic_slice_in_dim(cotangent, my_group * quarter, quarter, axis=1)
    x_buffer = jnp.where(filled[:, None], x_part[token_index], 0)
    dy_buffer = jnp.where(filled[:, None], dy_part[token_index], 0)
    gate_buffer = jnp.where(filled, gates.reshape(-1)[copy_index], 0)
    gate_cols = jnp.zeros((expert_count * capacity, 128), jnp.bfloat16).at[:, 0].set(gate_buffer)
    outgoing = jnp.concatenate([x_buffer, dy_buffer, gate_cols], axis=1)
    arrived = lax.all_to_all(outgoing, "expert", split_axis=0, concat_axis=0, tiled=True)
    stacked = jnp.concatenate([gate_weight, up_weight, down_weight], axis=1)
    moved, arrived = across_z(stacked, expert_count, groups, arrived)
    rows_per = gate_weight.shape[1]
    moved = (moved[:, :rows_per], moved[:, rows_per : 2 * rows_per], moved[:, 2 * rows_per :])
    weights = tuple(
        (jnp.where(own_flag == 1, fresh, stay) for fresh, stay in zip(moved, weights))
    )
    x_rows, dy_rows = dp_gather(arrived, groups, quarter)
    gate_rows = arrived[:, 2 * quarter]
    w_gate = weights[0][0]
    w_up = weights[1][0]
    w_down = weights[2][0]
    contract_last = (((1,), (1,)), ((), ()))
    pre_gate = lax.dot_general(x_rows, w_gate, contract_last, preferred_element_type=jnp.float32)
    pre_up = lax.dot_general(x_rows, w_up, contract_last, preferred_element_type=jnp.float32)
    sigma = jax.nn.sigmoid(pre_gate)
    active = pre_gate * sigma
    hidden = (active * pre_up).astype(jnp.bfloat16)
    back = lax.dot_general(dy_rows, w_down, contract_last, preferred_element_type=jnp.float32)
    score_part = jnp.sum(hidden.astype(jnp.float32) * back, axis=1)
    grad_hidden = gate_rows.astype(jnp.float32)[:, None] * back
    slope = sigma * (1.0 + pre_gate * (1.0 - sigma))
    grad_gate = (grad_hidden * pre_up * slope).astype(jnp.bfloat16)
    grad_up = (grad_hidden * active).astype(jnp.bfloat16)
    input_part = jnp.dot(grad_gate, w_gate, preferred_element_type=jnp.float32)
    input_part = input_part + jnp.dot(grad_up, w_up, preferred_element_type=jnp.float32)
    scaled = gate_rows[:, None] * dy_rows
    contract_rows = (((0,), (0,)), ((), ()))
    grad_wgate = lax.dot_general(
        grad_gate, x_rows, contract_rows, preferred_element_type=jnp.float32
    )
    grad_wup = lax.dot_general(grad_up, x_rows, contract_rows, preferred_element_type=jnp.float32)
    grad_wdown = lax.dot_general(hidden, scaled, contract_rows, preferred_element_type=jnp.float32)
    slots = capacity * expert_count
    score_tile = jnp.zeros((8 * 128,), jnp.float32).at[:slots].set(score_part).reshape(8, 128)
    share, score_sum = dp_scatter(input_part.astype(jnp.bfloat16), score_tile, groups)
    score_col = jnp.zeros((slots, 128), jnp.bfloat16).at[:, 0].set(
        score_sum.reshape(-1)[:slots].astype(jnp.bfloat16)
    )
    reduced = jnp.concatenate([share, score_col], axis=1)
    back_rows = lax.all_to_all(reduced, "expert", split_axis=0, concat_axis=0, tiled=True)
    per_copy = back_rows[buffer_index].reshape(row_count, routed, quarter + 128)
    input_grad = jnp.sum(per_copy[:, :, :quarter].astype(jnp.float32), axis=1).astype(jnp.bfloat16)
    gate_grad = per_copy[:, :, quarter]
    gradients = (
        grad_wgate.astype(jnp.bfloat16)[None],
        grad_wup.astype(jnp.bfloat16)[None],
        grad_wdown.astype(jnp.bfloat16)[None],
    )
    return (input_grad, gate_grad, gradients[0], gradients[1], gradients[2])


def solution(mesh):
    placed = (
        P("expert", None),
        P("expert", None),
        P("expert", "dp", None),
        P("expert", "dp", None),
        P("expert", "dp", None),
        P("expert", None),
        P("expert", None),
        P(),
    )
    return jax.shard_map(
        shards,
        mesh=mesh,
        in_specs=placed,
        out_specs=(
            P("expert", "dp"),
            P("expert", None),
            P("expert", "dp", None),
            P("expert", "dp", None),
            P("expert", "dp", None),
        ),
        check_vma=False,
    )
```

```python
import jax
import jax.numpy as jnp
from jax import lax
from jax.sharding import PartitionSpec as P
from jax.experimental import pallas as pl
from jax.experimental.pallas import tpu as pltpu

MESH_IDS = pl.DeviceIdType.MESH


def dp_scatter_kernel(groups, src_ref, score_ref, out_ref, score_out, landing, score_in, send_sem, recv_sem):
    me = lax.axis_index("dp")
    home = lax.axis_index("expert")
    width = landing.shape[2]
    barrier = pltpu.get_barrier_semaphore()
    for step in range(1, groups):
        peer = lax.rem(me + step, groups)
        pl.semaphore_signal(barrier, 1, device_id=(home, peer), device_id_type=MESH_IDS)
    pl.semaphore_wait(barrier, groups - 1)
    copies = []
    for step in range(1, groups):
        peer = lax.rem(me + step, groups)
        for part, (source, target) in enumerate(
            ((src_ref.at[:, pl.ds(pl.multiple_of(peer * width, 128), width)], landing), (score_ref, score_in))
        ):
            copy = pltpu.make_async_remote_copy(
                src_ref=source,
                dst_ref=target.at[step],
                send_sem=send_sem.at[step, part],
                recv_sem=recv_sem.at[step, part],
                device_id=(home, peer),
                device_id_type=MESH_IDS,
            )
            copy.start()
            copies.append(copy)
    for copy in copies:
        copy.wait()
    own = pl.multiple_of(me * width, 128)
    block = 64

    def body(i, carry):
        rows = pl.ds(pl.multiple_of(i * block, block), block)
        total = src_ref[rows, pl.ds(own, width)].astype(jnp.float32)
        for step in range(1, groups):
            total = total + landing[step, rows, :].astype(jnp.float32)
        out_ref[rows, :] = total.astype(out_ref.dtype)
        return carry

    lax.fori_loop(0, out_ref.shape[0] // block, body, 0)
    score = score_ref[...]
    for step in range(1, groups):
        score = score + score_in[step]
    score_out[...] = score


def dp_scatter(partial, score, groups):
    rows, full = partial.shape
    width = full // groups
    return pl.pallas_call(
        lambda *refs: dp_scatter_kernel(groups, *refs),
        out_shape=(
            jax.ShapeDtypeStruct((rows, width), partial.dtype),
            jax.ShapeDtypeStruct(score.shape, score.dtype),
        ),
        in_specs=[pl.BlockSpec(memory_space=pltpu.VMEM)] * 2,
        out_specs=(pl.BlockSpec(memory_space=pltpu.VMEM), pl.BlockSpec(memory_space=pltpu.VMEM)),
        scratch_shapes=[
            pltpu.VMEM((groups, rows, width), partial.dtype),
            pltpu.VMEM((groups,) + score.shape, score.dtype),
            pltpu.SemaphoreType.DMA((groups, 2)),
            pltpu.SemaphoreType.DMA((groups, 2)),
        ],
        compiler_params=pltpu.CompilerParams(collective_id=0, has_side_effects=True),
    )(partial, score)


def dp_gather_kernel(groups, width, src_ref, x_ref, dy_ref, local_sem, send_sem, recv_sem):
    me = lax.axis_index("dp")
    home = lax.axis_index("expert")
    barrier = pltpu.get_barrier_semaphore()
    for step in range(1, groups):
        peer = lax.rem(me + step, groups)
        pl.semaphore_signal(barrier, 1, device_id=(home, peer), device_id_type=MESH_IDS)
    pl.semaphore_wait(barrier, groups - 1)
    mine = pl.ds(pl.multiple_of(me * width, 128), width)
    copies = []
    for step in range(1, groups):
        peer = lax.rem(me + step, groups)
        for part, dst in enumerate((x_ref, dy_ref)):
            copy = pltpu.make_async_remote_copy(
                src_ref=src_ref.at[:, pl.ds(part * width, width)],
                dst_ref=dst.at[:, mine],
                send_sem=send_sem.at[step, part],
                recv_sem=recv_sem.at[step, part],
                device_id=(home, peer),
                device_id_type=MESH_IDS,
            )
            copy.start()
            copies.append(copy)
    for part, dst in enumerate((x_ref, dy_ref)):
        local = pltpu.make_async_copy(
            src_ref.at[:, pl.ds(part * width, width)], dst.at[:, mine], local_sem.at[part]
        )
        local.start()
        copies.append(local)
    for copy in copies:
        copy.wait()


def dp_gather(chunk, groups, width):
    rows = chunk.shape[0]
    full = jax.ShapeDtypeStruct((rows, groups * width), chunk.dtype)
    return pl.pallas_call(
        lambda *refs: dp_gather_kernel(groups, width, *refs),
        out_shape=(full, full),
        in_specs=[pl.BlockSpec(memory_space=pl.ANY)],
        out_specs=(pl.BlockSpec(memory_space=pl.ANY), pl.BlockSpec(memory_space=pl.ANY)),
        scratch_shapes=[
            pltpu.SemaphoreType.DMA((2,)),
            pltpu.SemaphoreType.DMA((groups, 2)),
            pltpu.SemaphoreType.DMA((groups, 2)),
        ],
        compiler_params=pltpu.CompilerParams(collective_id=2, has_side_effects=True),
    )(chunk)


def from_behind(value, axis, by):
    devices = lax.axis_size(axis)
    return lax.ppermute(value, axis, [(i, (i + by) % devices) for i in range(devices)])


def mirror_swap(value, expert_count, groups):
    half_axis = expert_count // 2
    pairs = [
        (slot * groups + group, ((slot + half_axis) % expert_count) * groups + groups - 1 - group)
        for slot in range(expert_count)
        for group in range(groups)
    ]
    return lax.ppermute(value, ("expert", "dp"), pairs)


def pair_lookup(experts, pair_flags, half_axis):
    match = experts[:, None] % half_axis == jnp.arange(half_axis, dtype=jnp.int32)[None, :]
    return jnp.sum(jnp.where(match, pair_flags[None, :], 0), axis=1)


def shards(tokens, cotangent, gate_weight, up_weight, down_weight, expert_ids, gates, swap_flags):
    expert_count = lax.axis_size("expert")
    half_axis = expert_count // 2
    my_slot = lax.axis_index("expert")
    row_count, model_width = tokens.shape
    routed = expert_ids.shape[1]
    capacity = row_count * routed * 5 // (4 * expert_count)
    groups = lax.axis_size("dp")
    quarter = model_width // groups
    own_flag = pair_lookup(jnp.reshape(my_slot, (1,)), swap_flags, half_axis)[0]
    flat_ids = expert_ids.reshape(-1)
    weights = (gate_weight, up_weight, down_weight)
    arrived = mirror_swap((gate_weight, up_weight, down_weight), expert_count, groups)
    weights = tuple(
        (jnp.where(own_flag == 1, fresh, stay) for fresh, stay in zip(arrived, weights))
    )
    flipped = pair_lookup(flat_ids, swap_flags, half_axis)
    target = jnp.where(flipped == 1, (flat_ids + half_axis) % expert_count, flat_ids)
    copies = row_count * routed
    onehot = (target[:, None] == jnp.arange(expert_count, dtype=jnp.int32)[None, :]).astype(
        jnp.int32
    )
    earlier = jnp.cumsum(onehot, axis=0) - onehot
    position = jnp.sum(earlier * onehot, axis=1)
    buffer_index = target * capacity + position
    source = jnp.zeros((expert_count * capacity,), jnp.int32)
    source = source.at[buffer_index].set(jnp.arange(copies, dtype=jnp.int32) + 1)
    filled = source > 0
    copy_index = jnp.maximum(source - 1, 0)
    token_index = copy_index // routed
    my_group = lax.axis_index("dp")
    x_part = lax.dynamic_slice_in_dim(tokens, my_group * quarter, quarter, axis=1)
    dy_part = lax.dynamic_slice_in_dim(cotangent, my_group * quarter, quarter, axis=1)
    x_buffer = jnp.where(filled[:, None], x_part[token_index], 0)
    dy_buffer = jnp.where(filled[:, None], dy_part[token_index], 0)
    gate_buffer = jnp.where(filled, gates.reshape(-1)[copy_index], 0)
    gate_cols = jnp.zeros((expert_count * capacity, 128), jnp.bfloat16).at[:, 0].set(gate_buffer)
    outgoing = jnp.concatenate([x_buffer, dy_buffer, gate_cols], axis=1)
    arrived = lax.all_to_all(outgoing, "expert", split_axis=0, concat_axis=0, tiled=True)
    x_rows, dy_rows = dp_gather(arrived, groups, quarter)
    gate_rows = arrived[:, 2 * quarter]
    w_gate = weights[0][0]
    w_up = weights[1][0]
    w_down = weights[2][0]
    contract_last = (((1,), (1,)), ((), ()))
    pre_gate = lax.dot_general(x_rows, w_gate, contract_last, preferred_element_type=jnp.float32)
    pre_up = lax.dot_general(x_rows, w_up, contract_last, preferred_element_type=jnp.float32)
    sigma = jax.nn.sigmoid(pre_gate)
    active = pre_gate * sigma
    hidden = (active * pre_up).astype(jnp.bfloat16)
    back = lax.dot_general(dy_rows, w_down, contract_last, preferred_element_type=jnp.float32)
    score_part = jnp.sum(hidden.astype(jnp.float32) * back, axis=1)
    grad_hidden = gate_rows.astype(jnp.float32)[:, None] * back
    slope = sigma * (1.0 + pre_gate * (1.0 - sigma))
    grad_gate = (grad_hidden * pre_up * slope).astype(jnp.bfloat16)
    grad_up = (grad_hidden * active).astype(jnp.bfloat16)
    input_part = jnp.dot(grad_gate, w_gate, preferred_element_type=jnp.float32)
    input_part = input_part + jnp.dot(grad_up, w_up, preferred_element_type=jnp.float32)
    scaled = gate_rows[:, None] * dy_rows
    contract_rows = (((0,), (0,)), ((), ()))
    computed = (grad_gate, grad_up, hidden)
    mirrored = lax.ppermute(computed, "dp", [(g, groups - 1 - g) for g in range(groups)])
    mine = tuple(jnp.where(own_flag == 1, far, near) for far, near in zip(mirrored, computed))
    grad_wgate = lax.dot_general(
        mine[0], x_rows, contract_rows, preferred_element_type=jnp.float32
    )
    grad_wup = lax.dot_general(mine[1], x_rows, contract_rows, preferred_element_type=jnp.float32)
    grad_wdown = lax.dot_general(mine[2], scaled, contract_rows, preferred_element_type=jnp.float32)
    slots = capacity * expert_count
    score_tile = jnp.zeros((8 * 128,), jnp.float32).at[:slots].set(score_part).reshape(8, 128)
    share, score_sum = dp_scatter(input_part.astype(jnp.bfloat16), score_tile, groups)
    score_col = jnp.zeros((slots, 128), jnp.bfloat16).at[:, 0].set(
        score_sum.reshape(-1)[:slots].astype(jnp.bfloat16)
    )
    reduced = jnp.concatenate([share, score_col], axis=1)
    back_rows = lax.all_to_all(reduced, "expert", split_axis=0, concat_axis=0, tiled=True)
    per_copy = back_rows[buffer_index].reshape(row_count, routed, quarter + 128)
    input_grad = jnp.sum(per_copy[:, :, :quarter].astype(jnp.float32), axis=1).astype(jnp.bfloat16)
    gate_grad = per_copy[:, :, quarter]
    gradients = (
        grad_wgate.astype(jnp.bfloat16)[None],
        grad_wup.astype(jnp.bfloat16)[None],
        grad_wdown.astype(jnp.bfloat16)[None],
    )
    return (input_grad, gate_grad, gradients[0], gradients[1], gradients[2])


def solution(mesh):
    placed = (
        P("expert", None),
        P("expert", None),
        P("expert", "dp", None),
        P("expert", "dp", None),
        P("expert", "dp", None),
        P("expert", None),
        P("expert", None),
        P(),
    )
    return jax.shard_map(
        shards,
        mesh=mesh,
        in_specs=placed,
        out_specs=(
            P("expert", "dp"),
            P("expert", None),
            P("expert", "dp", None),
            P("expert", "dp", None),
            P("expert", "dp", None),
        ),
        check_vma=False,
    )
```

```python
import jax
import jax.numpy as jnp
from jax import lax
from jax.sharding import PartitionSpec as P
from jax.experimental import pallas as pl
from jax.experimental.pallas import tpu as pltpu

MESH_IDS = pl.DeviceIdType.MESH


def dp_scatter_kernel(groups, src_ref, score_ref, out_ref, score_out, landing, score_in, send_sem, recv_sem):
    me = lax.axis_index("dp")
    home = lax.axis_index("expert")
    width = landing.shape[2]
    barrier = pltpu.get_barrier_semaphore()
    for step in range(1, groups):
        peer = lax.rem(me + step, groups)
        pl.semaphore_signal(barrier, 1, device_id=(home, peer), device_id_type=MESH_IDS)
    pl.semaphore_wait(barrier, groups - 1)
    copies = []
    for step in range(1, groups):
        peer = lax.rem(me + step, groups)
        for part, (source, target) in enumerate(
            ((src_ref.at[:, pl.ds(pl.multiple_of(peer * width, 128), width)], landing), (score_ref, score_in))
        ):
            copy = pltpu.make_async_remote_copy(
                src_ref=source,
                dst_ref=target.at[step],
                send_sem=send_sem.at[step, part],
                recv_sem=recv_sem.at[step, part],
                device_id=(home, peer),
                device_id_type=MESH_IDS,
            )
            copy.start()
            copies.append(copy)
    for copy in copies:
        copy.wait()
    own = pl.multiple_of(me * width, 128)
    block = 64

    def body(i, carry):
        rows = pl.ds(pl.multiple_of(i * block, block), block)
        total = src_ref[rows, pl.ds(own, width)].astype(jnp.float32)
        for step in range(1, groups):
            total = total + landing[step, rows, :].astype(jnp.float32)
        out_ref[rows, :] = total.astype(out_ref.dtype)
        return carry

    lax.fori_loop(0, out_ref.shape[0] // block, body, 0)
    score = score_ref[...]
    for step in range(1, groups):
        score = score + score_in[step]
    score_out[...] = score


def dp_scatter(partial, score, groups):
    rows, full = partial.shape
    width = full // groups
    return pl.pallas_call(
        lambda *refs: dp_scatter_kernel(groups, *refs),
        out_shape=(
            jax.ShapeDtypeStruct((rows, width), partial.dtype),
            jax.ShapeDtypeStruct(score.shape, score.dtype),
        ),
        in_specs=[pl.BlockSpec(memory_space=pltpu.VMEM)] * 2,
        out_specs=(pl.BlockSpec(memory_space=pltpu.VMEM), pl.BlockSpec(memory_space=pltpu.VMEM)),
        scratch_shapes=[
            pltpu.VMEM((groups, rows, width), partial.dtype),
            pltpu.VMEM((groups,) + score.shape, score.dtype),
            pltpu.SemaphoreType.DMA((groups, 2)),
            pltpu.SemaphoreType.DMA((groups, 2)),
        ],
        compiler_params=pltpu.CompilerParams(collective_id=0, has_side_effects=True),
    )(partial, score)


def dp_gather_kernel(groups, width, src_ref, x_ref, dy_ref, local_sem, send_sem, recv_sem):
    me = lax.axis_index("dp")
    home = lax.axis_index("expert")
    barrier = pltpu.get_barrier_semaphore()
    for step in range(1, groups):
        peer = lax.rem(me + step, groups)
        pl.semaphore_signal(barrier, 1, device_id=(home, peer), device_id_type=MESH_IDS)
    pl.semaphore_wait(barrier, groups - 1)
    mine = pl.ds(pl.multiple_of(me * width, 128), width)
    copies = []
    for step in range(1, groups):
        peer = lax.rem(me + step, groups)
        for part, dst in enumerate((x_ref, dy_ref)):
            copy = pltpu.make_async_remote_copy(
                src_ref=src_ref.at[:, pl.ds(part * width, width)],
                dst_ref=dst.at[:, mine],
                send_sem=send_sem.at[step, part],
                recv_sem=recv_sem.at[step, part],
                device_id=(home, peer),
                device_id_type=MESH_IDS,
            )
            copy.start()
            copies.append(copy)
    for part, dst in enumerate((x_ref, dy_ref)):
        local = pltpu.make_async_copy(
            src_ref.at[:, pl.ds(part * width, width)], dst.at[:, mine], local_sem.at[part]
        )
        local.start()
        copies.append(local)
    for copy in copies:
        copy.wait()


def dp_gather(chunk, groups, width):
    rows = chunk.shape[0]
    full = jax.ShapeDtypeStruct((rows, groups * width), chunk.dtype)
    return pl.pallas_call(
        lambda *refs: dp_gather_kernel(groups, width, *refs),
        out_shape=(full, full),
        in_specs=[pl.BlockSpec(memory_space=pl.ANY)],
        out_specs=(pl.BlockSpec(memory_space=pl.ANY), pl.BlockSpec(memory_space=pl.ANY)),
        scratch_shapes=[
            pltpu.SemaphoreType.DMA((2,)),
            pltpu.SemaphoreType.DMA((groups, 2)),
            pltpu.SemaphoreType.DMA((groups, 2)),
        ],
        compiler_params=pltpu.CompilerParams(collective_id=2, has_side_effects=True),
    )(chunk)


def from_behind(value, axis, by):
    devices = lax.axis_size(axis)
    return lax.ppermute(value, axis, [(i, (i + by) % devices) for i in range(devices)])


def mirror_swap(value, expert_count, groups):
    half_axis = expert_count // 2
    pairs = [
        (slot * groups + group, ((slot + half_axis) % expert_count) * groups + groups - 1 - group)
        for slot in range(expert_count)
        for group in range(groups)
    ]
    return lax.ppermute(value, ("expert", "dp"), pairs)


def pair_lookup(experts, pair_flags, half_axis):
    match = experts[:, None] % half_axis == jnp.arange(half_axis, dtype=jnp.int32)[None, :]
    return jnp.sum(jnp.where(match, pair_flags[None, :], 0), axis=1)


def shards(tokens, cotangent, gate_weight, up_weight, down_weight, expert_ids, gates, swap_flags):
    expert_count = lax.axis_size("expert")
    half_axis = expert_count // 2
    my_slot = lax.axis_index("expert")
    row_count, model_width = tokens.shape
    routed = expert_ids.shape[1]
    capacity = row_count * routed * 5 // (4 * expert_count)
    groups = lax.axis_size("dp")
    quarter = model_width // groups
    own_flag = pair_lookup(jnp.reshape(my_slot, (1,)), swap_flags, half_axis)[0]
    flat_ids = expert_ids.reshape(-1)
    weights = (gate_weight, up_weight, down_weight)
    arrived = mirror_swap((gate_weight, up_weight, down_weight), expert_count, groups)
    weights = tuple(
        (jnp.where(own_flag == 1, fresh, stay) for fresh, stay in zip(arrived, weights))
    )
    flipped = pair_lookup(flat_ids, swap_flags, half_axis)
    target = jnp.where(flipped == 1, (flat_ids + half_axis) % expert_count, flat_ids)
    copies = row_count * routed
    onehot = (target[:, None] == jnp.arange(expert_count, dtype=jnp.int32)[None, :]).astype(
        jnp.int32
    )
    earlier = jnp.cumsum(onehot, axis=0) - onehot
    position = jnp.sum(earlier * onehot, axis=1)
    buffer_index = target * capacity + position
    source = jnp.zeros((expert_count * capacity,), jnp.int32)
    source = source.at[buffer_index].set(jnp.arange(copies, dtype=jnp.int32) + 1)
    filled = source > 0
    copy_index = jnp.maximum(source - 1, 0)
    token_index = copy_index // routed
    my_group = lax.axis_index("dp")
    x_part = lax.dynamic_slice_in_dim(tokens, my_group * quarter, quarter, axis=1)
    dy_part = lax.dynamic_slice_in_dim(cotangent, my_group * quarter, quarter, axis=1)
    x_buffer = jnp.where(filled[:, None], x_part[token_index], 0)
    dy_buffer = jnp.where(filled[:, None], dy_part[token_index], 0)
    gate_buffer = jnp.where(filled, gates.reshape(-1)[copy_index], 0)
    gate_cols = jnp.zeros((expert_count * capacity, 128), jnp.bfloat16).at[:, 0].set(gate_buffer)
    outgoing = jnp.concatenate([x_buffer, dy_buffer, gate_cols], axis=1)
    arrived = lax.all_to_all(outgoing, "expert", split_axis=0, concat_axis=0, tiled=True)
    x_rows, dy_rows = dp_gather(arrived, groups, quarter)
    gate_rows = arrived[:, 2 * quarter]
    w_gate = weights[0][0]
    w_up = weights[1][0]
    w_down = weights[2][0]
    contract_last = (((1,), (1,)), ((), ()))
    pre_gate = lax.dot_general(x_rows, w_gate, contract_last, preferred_element_type=jnp.float32)
    pre_up = lax.dot_general(x_rows, w_up, contract_last, preferred_element_type=jnp.float32)
    sigma = jax.nn.sigmoid(pre_gate)
    active = pre_gate * sigma
    hidden = (active * pre_up).astype(jnp.bfloat16)
    back = lax.dot_general(dy_rows, w_down, contract_last, preferred_element_type=jnp.float32)
    score_part = jnp.sum(hidden.astype(jnp.float32) * back, axis=1)
    grad_hidden = gate_rows.astype(jnp.float32)[:, None] * back
    slope = sigma * (1.0 + pre_gate * (1.0 - sigma))
    grad_gate = (grad_hidden * pre_up * slope).astype(jnp.bfloat16)
    grad_up = (grad_hidden * active).astype(jnp.bfloat16)
    input_part = jnp.dot(grad_gate, w_gate, preferred_element_type=jnp.float32)
    input_part = input_part + jnp.dot(grad_up, w_up, preferred_element_type=jnp.float32)
    scaled = gate_rows[:, None] * dy_rows
    contract_rows = (((0,), (0,)), ((), ()))
    computed = (grad_gate, grad_up, hidden)
    mirrored = lax.ppermute(computed, "dp", [(g, groups - 1 - g) for g in range(groups)])
    mirrored, input_part, score_part = lax.optimization_barrier((mirrored, input_part, score_part))
    mine = tuple(jnp.where(own_flag == 1, far, near) for far, near in zip(mirrored, computed))
    grad_wgate = lax.dot_general(
        mine[0], x_rows, contract_rows, preferred_element_type=jnp.float32
    )
    grad_wup = lax.dot_general(mine[1], x_rows, contract_rows, preferred_element_type=jnp.float32)
    grad_wdown = lax.dot_general(mine[2], scaled, contract_rows, preferred_element_type=jnp.float32)
    slots = capacity * expert_count
    score_tile = jnp.zeros((8 * 128,), jnp.float32).at[:slots].set(score_part).reshape(8, 128)
    share, score_sum = dp_scatter(input_part.astype(jnp.bfloat16), score_tile, groups)
    score_col = jnp.zeros((slots, 128), jnp.bfloat16).at[:, 0].set(
        score_sum.reshape(-1)[:slots].astype(jnp.bfloat16)
    )
    reduced = jnp.concatenate([share, score_col], axis=1)
    back_rows = lax.all_to_all(reduced, "expert", split_axis=0, concat_axis=0, tiled=True)
    per_copy = back_rows[buffer_index].reshape(row_count, routed, quarter + 128)
    input_grad = jnp.sum(per_copy[:, :, :quarter].astype(jnp.float32), axis=1).astype(jnp.bfloat16)
    gate_grad = per_copy[:, :, quarter]
    gradients = (
        grad_wgate.astype(jnp.bfloat16)[None],
        grad_wup.astype(jnp.bfloat16)[None],
        grad_wdown.astype(jnp.bfloat16)[None],
    )
    return (input_grad, gate_grad, gradients[0], gradients[1], gradients[2])


def solution(mesh):
    placed = (
        P("expert", None),
        P("expert", None),
        P("expert", "dp", None),
        P("expert", "dp", None),
        P("expert", "dp", None),
        P("expert", None),
        P("expert", None),
        P(),
    )
    return jax.shard_map(
        shards,
        mesh=mesh,
        in_specs=placed,
        out_specs=(
            P("expert", "dp"),
            P("expert", None),
            P("expert", "dp", None),
            P("expert", "dp", None),
            P("expert", "dp", None),
        ),
        check_vma=False,
    )
```

```python
import jax
import jax.numpy as jnp
from jax import lax
from jax.sharding import PartitionSpec as P
from jax.experimental import pallas as pl
from jax.experimental.pallas import tpu as pltpu

MESH_IDS = pl.DeviceIdType.MESH


def dp_scatter_kernel(
    groups, src_ref, score_ref, grads_ref, out_ref, score_out, mirror_out, landing, score_in, send_sem, recv_sem, mirror_sem
):
    me = lax.axis_index("dp")
    home = lax.axis_index("expert")
    width = landing.shape[2]
    barrier = pltpu.get_barrier_semaphore()
    for step in range(1, groups):
        peer = lax.rem(me + step, groups)
        pl.semaphore_signal(barrier, 1, device_id=(home, peer), device_id_type=MESH_IDS)
    pl.semaphore_wait(barrier, groups - 1)
    copies = []
    for step in range(1, groups):
        peer = lax.rem(me + step, groups)
        for part, (source, target) in enumerate(
            ((src_ref.at[:, pl.ds(pl.multiple_of(peer * width, 128), width)], landing), (score_ref, score_in))
        ):
            copy = pltpu.make_async_remote_copy(
                src_ref=source,
                dst_ref=target.at[step],
                send_sem=send_sem.at[step, part],
                recv_sem=recv_sem.at[step, part],
                device_id=(home, peer),
                device_id_type=MESH_IDS,
            )
            copy.start()
            copies.append(copy)
    mirror = pltpu.make_async_remote_copy(
        src_ref=grads_ref,
        dst_ref=mirror_out,
        send_sem=mirror_sem.at[0],
        recv_sem=mirror_sem.at[1],
        device_id=(home, groups - 1 - me),
        device_id_type=MESH_IDS,
    )
    mirror.start()
    copies.append(mirror)
    for copy in copies:
        copy.wait()
    own = pl.multiple_of(me * width, 128)
    block = 64

    def body(i, carry):
        rows = pl.ds(pl.multiple_of(i * block, block), block)
        total = src_ref[rows, pl.ds(own, width)].astype(jnp.float32)
        for step in range(1, groups):
            total = total + landing[step, rows, :].astype(jnp.float32)
        out_ref[rows, :] = total.astype(out_ref.dtype)
        return carry

    lax.fori_loop(0, out_ref.shape[0] // block, body, 0)
    score = score_ref[...]
    for step in range(1, groups):
        score = score + score_in[step]
    score_out[...] = score


def dp_scatter(partial, score, grads, groups):
    rows, full = partial.shape
    width = full // groups
    return pl.pallas_call(
        lambda *refs: dp_scatter_kernel(groups, *refs),
        out_shape=(
            jax.ShapeDtypeStruct((rows, width), partial.dtype),
            jax.ShapeDtypeStruct(score.shape, score.dtype),
            jax.ShapeDtypeStruct(grads.shape, grads.dtype),
        ),
        in_specs=[pl.BlockSpec(memory_space=pltpu.VMEM)] * 3,
        out_specs=tuple(pl.BlockSpec(memory_space=pltpu.VMEM) for _ in range(3)),
        scratch_shapes=[
            pltpu.VMEM((groups, rows, width), partial.dtype),
            pltpu.VMEM((groups,) + score.shape, score.dtype),
            pltpu.SemaphoreType.DMA((groups, 2)),
            pltpu.SemaphoreType.DMA((groups, 2)),
            pltpu.SemaphoreType.DMA((2,)),
        ],
        compiler_params=pltpu.CompilerParams(collective_id=0, has_side_effects=True),
    )(partial, score, grads)


def dp_gather_kernel(groups, width, src_ref, x_ref, dy_ref, local_sem, send_sem, recv_sem):
    me = lax.axis_index("dp")
    home = lax.axis_index("expert")
    barrier = pltpu.get_barrier_semaphore()
    for step in range(1, groups):
        peer = lax.rem(me + step, groups)
        pl.semaphore_signal(barrier, 1, device_id=(home, peer), device_id_type=MESH_IDS)
    pl.semaphore_wait(barrier, groups - 1)
    mine = pl.ds(pl.multiple_of(me * width, 128), width)
    copies = []
    for step in range(1, groups):
        peer = lax.rem(me + step, groups)
        for part, dst in enumerate((x_ref, dy_ref)):
            copy = pltpu.make_async_remote_copy(
                src_ref=src_ref.at[:, pl.ds(part * width, width)],
                dst_ref=dst.at[:, mine],
                send_sem=send_sem.at[step, part],
                recv_sem=recv_sem.at[step, part],
                device_id=(home, peer),
                device_id_type=MESH_IDS,
            )
            copy.start()
            copies.append(copy)
    for part, dst in enumerate((x_ref, dy_ref)):
        local = pltpu.make_async_copy(
            src_ref.at[:, pl.ds(part * width, width)], dst.at[:, mine], local_sem.at[part]
        )
        local.start()
        copies.append(local)
    for copy in copies:
        copy.wait()


def dp_gather(chunk, groups, width):
    rows = chunk.shape[0]
    full = jax.ShapeDtypeStruct((rows, groups * width), chunk.dtype)
    return pl.pallas_call(
        lambda *refs: dp_gather_kernel(groups, width, *refs),
        out_shape=(full, full),
        in_specs=[pl.BlockSpec(memory_space=pl.ANY)],
        out_specs=(pl.BlockSpec(memory_space=pl.ANY), pl.BlockSpec(memory_space=pl.ANY)),
        scratch_shapes=[
            pltpu.SemaphoreType.DMA((2,)),
            pltpu.SemaphoreType.DMA((groups, 2)),
            pltpu.SemaphoreType.DMA((groups, 2)),
        ],
        compiler_params=pltpu.CompilerParams(collective_id=2, has_side_effects=True),
    )(chunk)


def from_behind(value, axis, by):
    devices = lax.axis_size(axis)
    return lax.ppermute(value, axis, [(i, (i + by) % devices) for i in range(devices)])


def mirror_swap(value, expert_count, groups):
    half_axis = expert_count // 2
    pairs = [
        (slot * groups + group, ((slot + half_axis) % expert_count) * groups + groups - 1 - group)
        for slot in range(expert_count)
        for group in range(groups)
    ]
    return lax.ppermute(value, ("expert", "dp"), pairs)


def pair_lookup(experts, pair_flags, half_axis):
    match = experts[:, None] % half_axis == jnp.arange(half_axis, dtype=jnp.int32)[None, :]
    return jnp.sum(jnp.where(match, pair_flags[None, :], 0), axis=1)


def shards(tokens, cotangent, gate_weight, up_weight, down_weight, expert_ids, gates, swap_flags):
    expert_count = lax.axis_size("expert")
    half_axis = expert_count // 2
    my_slot = lax.axis_index("expert")
    row_count, model_width = tokens.shape
    routed = expert_ids.shape[1]
    capacity = row_count * routed * 5 // (4 * expert_count)
    groups = lax.axis_size("dp")
    quarter = model_width // groups
    own_flag = pair_lookup(jnp.reshape(my_slot, (1,)), swap_flags, half_axis)[0]
    flat_ids = expert_ids.reshape(-1)
    weights = (gate_weight, up_weight, down_weight)
    arrived = mirror_swap((gate_weight, up_weight, down_weight), expert_count, groups)
    weights = tuple(
        (jnp.where(own_flag == 1, fresh, stay) for fresh, stay in zip(arrived, weights))
    )
    flipped = pair_lookup(flat_ids, swap_flags, half_axis)
    target = jnp.where(flipped == 1, (flat_ids + half_axis) % expert_count, flat_ids)
    copies = row_count * routed
    onehot = (target[:, None] == jnp.arange(expert_count, dtype=jnp.int32)[None, :]).astype(
        jnp.int32
    )
    earlier = jnp.cumsum(onehot, axis=0) - onehot
    position = jnp.sum(earlier * onehot, axis=1)
    buffer_index = target * capacity + position
    source = jnp.zeros((expert_count * capacity,), jnp.int32)
    source = source.at[buffer_index].set(jnp.arange(copies, dtype=jnp.int32) + 1)
    filled = source > 0
    copy_index = jnp.maximum(source - 1, 0)
    token_index = copy_index // routed
    my_group = lax.axis_index("dp")
    x_part = lax.dynamic_slice_in_dim(tokens, my_group * quarter, quarter, axis=1)
    dy_part = lax.dynamic_slice_in_dim(cotangent, my_group * quarter, quarter, axis=1)
    x_buffer = jnp.where(filled[:, None], x_part[token_index], 0)
    dy_buffer = jnp.where(filled[:, None], dy_part[token_index], 0)
    gate_buffer = jnp.where(filled, gates.reshape(-1)[copy_index], 0)
    gate_cols = jnp.zeros((expert_count * capacity, 128), jnp.bfloat16).at[:, 0].set(gate_buffer)
    outgoing = jnp.concatenate([x_buffer, dy_buffer, gate_cols], axis=1)
    arrived = lax.all_to_all(outgoing, "expert", split_axis=0, concat_axis=0, tiled=True)
    x_rows, dy_rows = dp_gather(arrived, groups, quarter)
    gate_rows = arrived[:, 2 * quarter]
    w_gate = weights[0][0]
    w_up = weights[1][0]
    w_down = weights[2][0]
    contract_last = (((1,), (1,)), ((), ()))
    pre_gate = lax.dot_general(x_rows, w_gate, contract_last, preferred_element_type=jnp.float32)
    pre_up = lax.dot_general(x_rows, w_up, contract_last, preferred_element_type=jnp.float32)
    sigma = jax.nn.sigmoid(pre_gate)
    active = pre_gate * sigma
    hidden = (active * pre_up).astype(jnp.bfloat16)
    back = lax.dot_general(dy_rows, w_down, contract_last, preferred_element_type=jnp.float32)
    score_part = jnp.sum(hidden.astype(jnp.float32) * back, axis=1)
    grad_hidden = gate_rows.astype(jnp.float32)[:, None] * back
    slope = sigma * (1.0 + pre_gate * (1.0 - sigma))
    grad_gate = (grad_hidden * pre_up * slope).astype(jnp.bfloat16)
    grad_up = (grad_hidden * active).astype(jnp.bfloat16)
    input_part = jnp.dot(grad_gate, w_gate, preferred_element_type=jnp.float32)
    input_part = input_part + jnp.dot(grad_up, w_up, preferred_element_type=jnp.float32)
    scaled = gate_rows[:, None] * dy_rows
    contract_rows = (((0,), (0,)), ((), ()))
    computed = (grad_gate, grad_up, hidden)
    slots = capacity * expert_count
    score_tile = jnp.zeros((8 * 128,), jnp.float32).at[:slots].set(score_part).reshape(8, 128)
    share, score_sum, mirrored = dp_scatter(
        input_part.astype(jnp.bfloat16), score_tile, jnp.stack(computed), groups
    )
    mine = tuple(jnp.where(own_flag == 1, mirrored[k], computed[k]) for k in range(3))
    grad_wgate = lax.dot_general(
        mine[0], x_rows, contract_rows, preferred_element_type=jnp.float32
    )
    grad_wup = lax.dot_general(mine[1], x_rows, contract_rows, preferred_element_type=jnp.float32)
    grad_wdown = lax.dot_general(mine[2], scaled, contract_rows, preferred_element_type=jnp.float32)
    score_col = jnp.zeros((slots, 128), jnp.bfloat16).at[:, 0].set(
        score_sum.reshape(-1)[:slots].astype(jnp.bfloat16)
    )
    reduced = jnp.concatenate([share, score_col], axis=1)
    back_rows = lax.all_to_all(reduced, "expert", split_axis=0, concat_axis=0, tiled=True)
    per_copy = back_rows[buffer_index].reshape(row_count, routed, quarter + 128)
    input_grad = jnp.sum(per_copy[:, :, :quarter].astype(jnp.float32), axis=1).astype(jnp.bfloat16)
    gate_grad = per_copy[:, :, quarter]
    gradients = (
        grad_wgate.astype(jnp.bfloat16)[None],
        grad_wup.astype(jnp.bfloat16)[None],
        grad_wdown.astype(jnp.bfloat16)[None],
    )
    return (input_grad, gate_grad, gradients[0], gradients[1], gradients[2])


def solution(mesh):
    placed = (
        P("expert", None),
        P("expert", None),
        P("expert", "dp", None),
        P("expert", "dp", None),
        P("expert", "dp", None),
        P("expert", None),
        P("expert", None),
        P(),
    )
    return jax.shard_map(
        shards,
        mesh=mesh,
        in_specs=placed,
        out_specs=(
            P("expert", "dp"),
            P("expert", None),
            P("expert", "dp", None),
            P("expert", "dp", None),
            P("expert", "dp", None),
        ),
        check_vma=False,
    )
```

```python
import jax
import jax.numpy as jnp
from jax import lax
from jax.sharding import PartitionSpec as P
from jax.experimental import pallas as pl
from jax.experimental.pallas import tpu as pltpu

MESH_IDS = pl.DeviceIdType.MESH


def dp_scatter_kernel(
    groups, src_ref, score_ref, grads_ref, out_ref, score_out, mirror_out, landing, score_in, send_sem, recv_sem, mirror_sem
):
    me = lax.axis_index("dp")
    home = lax.axis_index("expert")
    width = landing.shape[2]
    barrier = pltpu.get_barrier_semaphore()
    for step in range(1, groups):
        peer = lax.rem(me + step, groups)
        pl.semaphore_signal(barrier, 1, device_id=(home, peer), device_id_type=MESH_IDS)
    pl.semaphore_wait(barrier, groups - 1)
    copies = []
    for step in range(1, groups):
        peer = lax.rem(me + step, groups)
        for part, (source, target) in enumerate(
            ((src_ref.at[:, pl.ds(pl.multiple_of(peer * width, 128), width)], landing), (score_ref, score_in))
        ):
            copy = pltpu.make_async_remote_copy(
                src_ref=source,
                dst_ref=target.at[step],
                send_sem=send_sem.at[step, part],
                recv_sem=recv_sem.at[step, part],
                device_id=(home, peer),
                device_id_type=MESH_IDS,
            )
            copy.start()
            copies.append(copy)
    mirror = pltpu.make_async_remote_copy(
        src_ref=grads_ref,
        dst_ref=mirror_out,
        send_sem=mirror_sem.at[0],
        recv_sem=mirror_sem.at[1],
        device_id=(home, groups - 1 - me),
        device_id_type=MESH_IDS,
    )
    mirror.start()
    copies.append(mirror)
    for copy in copies:
        copy.wait()
    own = pl.multiple_of(me * width, 128)
    block = 64

    def body(i, carry):
        rows = pl.ds(pl.multiple_of(i * block, block), block)
        total = src_ref[rows, pl.ds(own, width)].astype(jnp.float32)
        for step in range(1, groups):
            total = total + landing[step, rows, :].astype(jnp.float32)
        out_ref[rows, :] = total.astype(out_ref.dtype)
        return carry

    lax.fori_loop(0, out_ref.shape[0] // block, body, 0)
    score = score_ref[...]
    for step in range(1, groups):
        score = score + score_in[step]
    score_out[...] = score


def dp_scatter(partial, score, grads, groups):
    rows, full = partial.shape
    width = full // groups
    return pl.pallas_call(
        lambda *refs: dp_scatter_kernel(groups, *refs),
        out_shape=(
            jax.ShapeDtypeStruct((rows, width), partial.dtype),
            jax.ShapeDtypeStruct(score.shape, score.dtype),
            jax.ShapeDtypeStruct(grads.shape, grads.dtype),
        ),
        in_specs=[pl.BlockSpec(memory_space=pltpu.VMEM)] * 3,
        out_specs=tuple(pl.BlockSpec(memory_space=pltpu.VMEM) for _ in range(3)),
        scratch_shapes=[
            pltpu.VMEM((groups, rows, width), partial.dtype),
            pltpu.VMEM((groups,) + score.shape, score.dtype),
            pltpu.SemaphoreType.DMA((groups, 2)),
            pltpu.SemaphoreType.DMA((groups, 2)),
            pltpu.SemaphoreType.DMA((2,)),
        ],
        compiler_params=pltpu.CompilerParams(collective_id=0, has_side_effects=True),
    )(partial, score, grads)


def dp_gather_kernel(groups, width, src_ref, x_ref, dy_ref, local_sem, send_sem, recv_sem):
    me = lax.axis_index("dp")
    home = lax.axis_index("expert")
    barrier = pltpu.get_barrier_semaphore()
    for step in range(1, groups):
        peer = lax.rem(me + step, groups)
        pl.semaphore_signal(barrier, 1, device_id=(home, peer), device_id_type=MESH_IDS)
    pl.semaphore_wait(barrier, groups - 1)
    mine = pl.ds(pl.multiple_of(me * width, 128), width)
    copies = []
    for step in range(1, groups):
        peer = lax.rem(me + step, groups)
        for part, dst in enumerate((x_ref, dy_ref)):
            copy = pltpu.make_async_remote_copy(
                src_ref=src_ref.at[:, pl.ds(part * width, width)],
                dst_ref=dst.at[:, mine],
                send_sem=send_sem.at[step, part],
                recv_sem=recv_sem.at[step, part],
                device_id=(home, peer),
                device_id_type=MESH_IDS,
            )
            copy.start()
            copies.append(copy)
    for part, dst in enumerate((x_ref, dy_ref)):
        local = pltpu.make_async_copy(
            src_ref.at[:, pl.ds(part * width, width)], dst.at[:, mine], local_sem.at[part]
        )
        local.start()
        copies.append(local)
    for copy in copies:
        copy.wait()


def dp_gather(chunk, groups, width):
    rows = chunk.shape[0]
    full = jax.ShapeDtypeStruct((rows, groups * width), chunk.dtype)
    return pl.pallas_call(
        lambda *refs: dp_gather_kernel(groups, width, *refs),
        out_shape=(full, full),
        in_specs=[pl.BlockSpec(memory_space=pl.ANY)],
        out_specs=(pl.BlockSpec(memory_space=pl.ANY), pl.BlockSpec(memory_space=pl.ANY)),
        scratch_shapes=[
            pltpu.SemaphoreType.DMA((2,)),
            pltpu.SemaphoreType.DMA((groups, 2)),
            pltpu.SemaphoreType.DMA((groups, 2)),
        ],
        compiler_params=pltpu.CompilerParams(collective_id=2, has_side_effects=True),
    )(chunk)


def from_behind(value, axis, by):
    devices = lax.axis_size(axis)
    return lax.ppermute(value, axis, [(i, (i + by) % devices) for i in range(devices)])


def mirror_swap(value, expert_count, groups):
    half_axis = expert_count // 2
    pairs = [
        (slot * groups + group, ((slot + half_axis) % expert_count) * groups + groups - 1 - group)
        for slot in range(expert_count)
        for group in range(groups)
    ]
    return lax.ppermute(value, ("expert", "dp"), pairs)


def pair_lookup(experts, pair_flags, half_axis):
    match = experts[:, None] % half_axis == jnp.arange(half_axis, dtype=jnp.int32)[None, :]
    return jnp.sum(jnp.where(match, pair_flags[None, :], 0), axis=1)


def shards(tokens, cotangent, gate_weight, up_weight, down_weight, expert_ids, gates, swap_flags):
    expert_count = lax.axis_size("expert")
    half_axis = expert_count // 2
    my_slot = lax.axis_index("expert")
    row_count, model_width = tokens.shape
    routed = expert_ids.shape[1]
    capacity = row_count * routed * 5 // (4 * expert_count)
    groups = lax.axis_size("dp")
    quarter = model_width // groups
    own_flag = pair_lookup(jnp.reshape(my_slot, (1,)), swap_flags, half_axis)[0]
    flat_ids = expert_ids.reshape(-1)
    flipped = pair_lookup(flat_ids, swap_flags, half_axis)
    target = jnp.where(flipped == 1, (flat_ids + half_axis) % expert_count, flat_ids)
    copies = row_count * routed
    onehot = (target[:, None] == jnp.arange(expert_count, dtype=jnp.int32)[None, :]).astype(
        jnp.int32
    )
    earlier = jnp.cumsum(onehot, axis=0) - onehot
    position = jnp.sum(earlier * onehot, axis=1)
    buffer_index = target * capacity + position
    source = jnp.zeros((expert_count * capacity,), jnp.int32)
    source = source.at[buffer_index].set(jnp.arange(copies, dtype=jnp.int32) + 1)
    filled = source > 0
    copy_index = jnp.maximum(source - 1, 0)
    token_index = copy_index // routed
    my_group = lax.axis_index("dp")
    x_part = lax.dynamic_slice_in_dim(tokens, my_group * quarter, quarter, axis=1)
    dy_part = lax.dynamic_slice_in_dim(cotangent, my_group * quarter, quarter, axis=1)
    x_buffer = jnp.where(filled[:, None], x_part[token_index], 0)
    dy_buffer = jnp.where(filled[:, None], dy_part[token_index], 0)
    gate_buffer = jnp.where(filled, gates.reshape(-1)[copy_index], 0)
    gate_cols = jnp.zeros((expert_count * capacity, 128), jnp.bfloat16).at[:, 0].set(gate_buffer)
    outgoing = jnp.concatenate([x_buffer, dy_buffer, gate_cols], axis=1)
    arrived = lax.all_to_all(outgoing, "expert", split_axis=0, concat_axis=0, tiled=True)
    weights = (gate_weight, up_weight, down_weight)
    held, arrived = lax.optimization_barrier((weights, arrived))
    moved = mirror_swap(held, expert_count, groups)
    weights = tuple(
        (jnp.where(own_flag == 1, fresh, stay) for fresh, stay in zip(moved, weights))
    )
    x_rows, dy_rows = dp_gather(arrived, groups, quarter)
    gate_rows = arrived[:, 2 * quarter]
    w_gate = weights[0][0]
    w_up = weights[1][0]
    w_down = weights[2][0]
    contract_last = (((1,), (1,)), ((), ()))
    pre_gate = lax.dot_general(x_rows, w_gate, contract_last, preferred_element_type=jnp.float32)
    pre_up = lax.dot_general(x_rows, w_up, contract_last, preferred_element_type=jnp.float32)
    sigma = jax.nn.sigmoid(pre_gate)
    active = pre_gate * sigma
    hidden = (active * pre_up).astype(jnp.bfloat16)
    back = lax.dot_general(dy_rows, w_down, contract_last, preferred_element_type=jnp.float32)
    score_part = jnp.sum(hidden.astype(jnp.float32) * back, axis=1)
    grad_hidden = gate_rows.astype(jnp.float32)[:, None] * back
    slope = sigma * (1.0 + pre_gate * (1.0 - sigma))
    grad_gate = (grad_hidden * pre_up * slope).astype(jnp.bfloat16)
    grad_up = (grad_hidden * active).astype(jnp.bfloat16)
    input_part = jnp.dot(grad_gate, w_gate, preferred_element_type=jnp.float32)
    input_part = input_part + jnp.dot(grad_up, w_up, preferred_element_type=jnp.float32)
    scaled = gate_rows[:, None] * dy_rows
    contract_rows = (((0,), (0,)), ((), ()))
    computed = (grad_gate, grad_up, hidden)
    slots = capacity * expert_count
    score_tile = jnp.zeros((8 * 128,), jnp.float32).at[:slots].set(score_part).reshape(8, 128)
    share, score_sum, mirrored = dp_scatter(
        input_part.astype(jnp.bfloat16), score_tile, jnp.stack(computed), groups
    )
    mine = tuple(jnp.where(own_flag == 1, mirrored[k], computed[k]) for k in range(3))
    grad_wgate = lax.dot_general(
        mine[0], x_rows, contract_rows, preferred_element_type=jnp.float32
    )
    grad_wup = lax.dot_general(mine[1], x_rows, contract_rows, preferred_element_type=jnp.float32)
    grad_wdown = lax.dot_general(mine[2], scaled, contract_rows, preferred_element_type=jnp.float32)
    score_col = jnp.zeros((slots, 128), jnp.bfloat16).at[:, 0].set(
        score_sum.reshape(-1)[:slots].astype(jnp.bfloat16)
    )
    reduced = jnp.concatenate([share, score_col], axis=1)
    back_rows = lax.all_to_all(reduced, "expert", split_axis=0, concat_axis=0, tiled=True)
    per_copy = back_rows[buffer_index].reshape(row_count, routed, quarter + 128)
    input_grad = jnp.sum(per_copy[:, :, :quarter].astype(jnp.float32), axis=1).astype(jnp.bfloat16)
    gate_grad = per_copy[:, :, quarter]
    gradients = (
        grad_wgate.astype(jnp.bfloat16)[None],
        grad_wup.astype(jnp.bfloat16)[None],
        grad_wdown.astype(jnp.bfloat16)[None],
    )
    return (input_grad, gate_grad, gradients[0], gradients[1], gradients[2])


def solution(mesh):
    placed = (
        P("expert", None),
        P("expert", None),
        P("expert", "dp", None),
        P("expert", "dp", None),
        P("expert", "dp", None),
        P("expert", None),
        P("expert", None),
        P(),
    )
    return jax.shard_map(
        shards,
        mesh=mesh,
        in_specs=placed,
        out_specs=(
            P("expert", "dp"),
            P("expert", None),
            P("expert", "dp", None),
            P("expert", "dp", None),
            P("expert", "dp", None),
        ),
        check_vma=False,
    )
```

```python
import jax
import jax.numpy as jnp
from jax import lax
from jax.sharding import PartitionSpec as P
from jax.experimental import pallas as pl
from jax.experimental.pallas import tpu as pltpu

MESH_IDS = pl.DeviceIdType.MESH


def dp_scatter_kernel(
    groups, src_ref, score_ref, grads_ref, out_ref, score_out, mirror_out, landing, score_in, send_sem, recv_sem, mirror_sem
):
    me = lax.axis_index("dp")
    home = lax.axis_index("expert")
    width = landing.shape[2]
    barrier = pltpu.get_barrier_semaphore()
    for step in range(1, groups):
        peer = lax.rem(me + step, groups)
        pl.semaphore_signal(barrier, 1, device_id=(home, peer), device_id_type=MESH_IDS)
    pl.semaphore_wait(barrier, groups - 1)
    copies = []
    far = (groups - 1) * (1 - me // 2)
    middle = lax.rem(3 * me + 2, 5)
    for peer in (far, middle, groups * (groups - 1) // 2 - me - far - middle):
        step = lax.rem(peer - me + groups, groups)
        for part, (source, target) in enumerate(
            ((src_ref.at[:, pl.ds(pl.multiple_of(peer * width, 128), width)], landing), (score_ref, score_in))
        ):
            copy = pltpu.make_async_remote_copy(
                src_ref=source,
                dst_ref=target.at[step],
                send_sem=send_sem.at[step, part],
                recv_sem=recv_sem.at[step, part],
                device_id=(home, peer),
                device_id_type=MESH_IDS,
            )
            copy.start()
            copies.append(copy)
    mirror = pltpu.make_async_remote_copy(
        src_ref=grads_ref,
        dst_ref=mirror_out,
        send_sem=mirror_sem.at[0],
        recv_sem=mirror_sem.at[1],
        device_id=(home, groups - 1 - me),
        device_id_type=MESH_IDS,
    )
    mirror.start()
    copies.append(mirror)
    for copy in copies:
        copy.wait()
    own = pl.multiple_of(me * width, 128)
    block = 64

    def body(i, carry):
        rows = pl.ds(pl.multiple_of(i * block, block), block)
        total = src_ref[rows, pl.ds(own, width)].astype(jnp.float32)
        for step in range(1, groups):
            total = total + landing[step, rows, :].astype(jnp.float32)
        out_ref[rows, :] = total.astype(out_ref.dtype)
        return carry

    lax.fori_loop(0, out_ref.shape[0] // block, body, 0)
    score = score_ref[...]
    for step in range(1, groups):
        score = score + score_in[step]
    score_out[...] = score


def dp_scatter(partial, score, grads, groups):
    rows, full = partial.shape
    width = full // groups
    return pl.pallas_call(
        lambda *refs: dp_scatter_kernel(groups, *refs),
        out_shape=(
            jax.ShapeDtypeStruct((rows, width), partial.dtype),
            jax.ShapeDtypeStruct(score.shape, score.dtype),
            jax.ShapeDtypeStruct(grads.shape, grads.dtype),
        ),
        in_specs=[pl.BlockSpec(memory_space=pltpu.VMEM)] * 3,
        out_specs=tuple(pl.BlockSpec(memory_space=pltpu.VMEM) for _ in range(3)),
        scratch_shapes=[
            pltpu.VMEM((groups, rows, width), partial.dtype),
            pltpu.VMEM((groups,) + score.shape, score.dtype),
            pltpu.SemaphoreType.DMA((groups, 2)),
            pltpu.SemaphoreType.DMA((groups, 2)),
            pltpu.SemaphoreType.DMA((2,)),
        ],
        compiler_params=pltpu.CompilerParams(collective_id=0, has_side_effects=True),
    )(partial, score, grads)


def dp_gather_kernel(groups, width, src_ref, x_ref, dy_ref, local_sem, send_sem, recv_sem):
    me = lax.axis_index("dp")
    home = lax.axis_index("expert")
    barrier = pltpu.get_barrier_semaphore()
    for step in range(1, groups):
        peer = lax.rem(me + step, groups)
        pl.semaphore_signal(barrier, 1, device_id=(home, peer), device_id_type=MESH_IDS)
    pl.semaphore_wait(barrier, groups - 1)
    mine = pl.ds(pl.multiple_of(me * width, 128), width)
    copies = []
    for step in range(1, groups):
        peer = lax.rem(me + step, groups)
        for part, dst in enumerate((x_ref, dy_ref)):
            copy = pltpu.make_async_remote_copy(
                src_ref=src_ref.at[:, pl.ds(part * width, width)],
                dst_ref=dst.at[:, mine],
                send_sem=send_sem.at[step, part],
                recv_sem=recv_sem.at[step, part],
                device_id=(home, peer),
                device_id_type=MESH_IDS,
            )
            copy.start()
            copies.append(copy)
    for part, dst in enumerate((x_ref, dy_ref)):
        local = pltpu.make_async_copy(
            src_ref.at[:, pl.ds(part * width, width)], dst.at[:, mine], local_sem.at[part]
        )
        local.start()
        copies.append(local)
    for copy in copies:
        copy.wait()


def dp_gather(chunk, groups, width):
    rows = chunk.shape[0]
    full = jax.ShapeDtypeStruct((rows, groups * width), chunk.dtype)
    return pl.pallas_call(
        lambda *refs: dp_gather_kernel(groups, width, *refs),
        out_shape=(full, full),
        in_specs=[pl.BlockSpec(memory_space=pl.ANY)],
        out_specs=(pl.BlockSpec(memory_space=pl.ANY), pl.BlockSpec(memory_space=pl.ANY)),
        scratch_shapes=[
            pltpu.SemaphoreType.DMA((2,)),
            pltpu.SemaphoreType.DMA((groups, 2)),
            pltpu.SemaphoreType.DMA((groups, 2)),
        ],
        compiler_params=pltpu.CompilerParams(collective_id=2, has_side_effects=True),
    )(chunk)


def from_behind(value, axis, by):
    devices = lax.axis_size(axis)
    return lax.ppermute(value, axis, [(i, (i + by) % devices) for i in range(devices)])


def mirror_swap(value, expert_count, groups):
    half_axis = expert_count // 2
    pairs = [
        (slot * groups + group, ((slot + half_axis) % expert_count) * groups + groups - 1 - group)
        for slot in range(expert_count)
        for group in range(groups)
    ]
    return lax.ppermute(value, ("expert", "dp"), pairs)


def pair_lookup(experts, pair_flags, half_axis):
    match = experts[:, None] % half_axis == jnp.arange(half_axis, dtype=jnp.int32)[None, :]
    return jnp.sum(jnp.where(match, pair_flags[None, :], 0), axis=1)


def shards(tokens, cotangent, gate_weight, up_weight, down_weight, expert_ids, gates, swap_flags):
    expert_count = lax.axis_size("expert")
    half_axis = expert_count // 2
    my_slot = lax.axis_index("expert")
    row_count, model_width = tokens.shape
    routed = expert_ids.shape[1]
    capacity = row_count * routed * 5 // (4 * expert_count)
    groups = lax.axis_size("dp")
    quarter = model_width // groups
    own_flag = pair_lookup(jnp.reshape(my_slot, (1,)), swap_flags, half_axis)[0]
    flat_ids = expert_ids.reshape(-1)
    flipped = pair_lookup(flat_ids, swap_flags, half_axis)
    target = jnp.where(flipped == 1, (flat_ids + half_axis) % expert_count, flat_ids)
    copies = row_count * routed
    onehot = (target[:, None] == jnp.arange(expert_count, dtype=jnp.int32)[None, :]).astype(
        jnp.int32
    )
    earlier = jnp.cumsum(onehot, axis=0) - onehot
    position = jnp.sum(earlier * onehot, axis=1)
    buffer_index = target * capacity + position
    source = jnp.zeros((expert_count * capacity,), jnp.int32)
    source = source.at[buffer_index].set(jnp.arange(copies, dtype=jnp.int32) + 1)
    filled = source > 0
    copy_index = jnp.maximum(source - 1, 0)
    token_index = copy_index // routed
    my_group = lax.axis_index("dp")
    x_part = lax.dynamic_slice_in_dim(tokens, my_group * quarter, quarter, axis=1)
    dy_part = lax.dynamic_slice_in_dim(cotangent, my_group * quarter, quarter, axis=1)
    x_buffer = jnp.where(filled[:, None], x_part[token_index], 0)
    dy_buffer = jnp.where(filled[:, None], dy_part[token_index], 0)
    gate_buffer = jnp.where(filled, gates.reshape(-1)[copy_index], 0)
    gate_cols = jnp.zeros((expert_count * capacity, 128), jnp.bfloat16).at[:, 0].set(gate_buffer)
    outgoing = jnp.concatenate([x_buffer, dy_buffer, gate_cols], axis=1)
    arrived = lax.all_to_all(outgoing, "expert", split_axis=0, concat_axis=0, tiled=True)
    weights = (gate_weight, up_weight, down_weight)
    held, arrived = lax.optimization_barrier((weights, arrived))
    moved = mirror_swap(held, expert_count, groups)
    weights = tuple(
        (jnp.where(own_flag == 1, fresh, stay) for fresh, stay in zip(moved, weights))
    )
    x_rows, dy_rows = dp_gather(arrived, groups, quarter)
    gate_rows = arrived[:, 2 * quarter]
    w_gate = weights[0][0]
    w_up = weights[1][0]
    w_down = weights[2][0]
    contract_last = (((1,), (1,)), ((), ()))
    pre_gate = lax.dot_general(x_rows, w_gate, contract_last, preferred_element_type=jnp.float32)
    pre_up = lax.dot_general(x_rows, w_up, contract_last, preferred_element_type=jnp.float32)
    sigma = jax.nn.sigmoid(pre_gate)
    active = pre_gate * sigma
    hidden = (active * pre_up).astype(jnp.bfloat16)
    back = lax.dot_general(dy_rows, w_down, contract_last, preferred_element_type=jnp.float32)
    score_part = jnp.sum(hidden.astype(jnp.float32) * back, axis=1)
    grad_hidden = gate_rows.astype(jnp.float32)[:, None] * back
    slope = sigma * (1.0 + pre_gate * (1.0 - sigma))
    grad_gate = (grad_hidden * pre_up * slope).astype(jnp.bfloat16)
    grad_up = (grad_hidden * active).astype(jnp.bfloat16)
    input_part = jnp.dot(grad_gate, w_gate, preferred_element_type=jnp.float32)
    input_part = input_part + jnp.dot(grad_up, w_up, preferred_element_type=jnp.float32)
    scaled = gate_rows[:, None] * dy_rows
    contract_rows = (((0,), (0,)), ((), ()))
    computed = (grad_gate, grad_up, hidden)
    slots = capacity * expert_count
    score_tile = jnp.zeros((8 * 128,), jnp.float32).at[:slots].set(score_part).reshape(8, 128)
    share, score_sum, mirrored = dp_scatter(
        input_part.astype(jnp.bfloat16), score_tile, jnp.stack(computed), groups
    )
    mine = tuple(jnp.where(own_flag == 1, mirrored[k], computed[k]) for k in range(3))
    grad_wgate = lax.dot_general(
        mine[0], x_rows, contract_rows, preferred_element_type=jnp.float32
    )
    grad_wup = lax.dot_general(mine[1], x_rows, contract_rows, preferred_element_type=jnp.float32)
    grad_wdown = lax.dot_general(mine[2], scaled, contract_rows, preferred_element_type=jnp.float32)
    score_col = jnp.zeros((slots, 128), jnp.bfloat16).at[:, 0].set(
        score_sum.reshape(-1)[:slots].astype(jnp.bfloat16)
    )
    reduced = jnp.concatenate([share, score_col], axis=1)
    back_rows = lax.all_to_all(reduced, "expert", split_axis=0, concat_axis=0, tiled=True)
    per_copy = back_rows[buffer_index].reshape(row_count, routed, quarter + 128)
    input_grad = jnp.sum(per_copy[:, :, :quarter].astype(jnp.float32), axis=1).astype(jnp.bfloat16)
    gate_grad = per_copy[:, :, quarter]
    gradients = (
        grad_wgate.astype(jnp.bfloat16)[None],
        grad_wup.astype(jnp.bfloat16)[None],
        grad_wdown.astype(jnp.bfloat16)[None],
    )
    return (input_grad, gate_grad, gradients[0], gradients[1], gradients[2])


def solution(mesh):
    placed = (
        P("expert", None),
        P("expert", None),
        P("expert", "dp", None),
        P("expert", "dp", None),
        P("expert", "dp", None),
        P("expert", None),
        P("expert", None),
        P(),
    )
    return jax.shard_map(
        shards,
        mesh=mesh,
        in_specs=placed,
        out_specs=(
            P("expert", "dp"),
            P("expert", None),
            P("expert", "dp", None),
            P("expert", "dp", None),
            P("expert", "dp", None),
        ),
        check_vma=False,
    )
```

```python
import jax
import jax.numpy as jnp
from jax import lax
from jax.sharding import PartitionSpec as P
from jax.experimental import pallas as pl
from jax.experimental.pallas import tpu as pltpu

MESH_IDS = pl.DeviceIdType.MESH


def dp_scatter_kernel(
    groups, src_ref, score_ref, grads_ref, out_ref, score_out, mirror_out, landing, score_in, send_sem, recv_sem, mirror_sem
):
    me = lax.axis_index("dp")
    home = lax.axis_index("expert")
    width = landing.shape[2]
    barrier = pltpu.get_barrier_semaphore()
    for step in range(1, groups):
        peer = lax.rem(me + step, groups)
        pl.semaphore_signal(barrier, 1, device_id=(home, peer), device_id_type=MESH_IDS)
    pl.semaphore_wait(barrier, groups - 1)
    copies = []
    far = (groups - 1) * (1 - me // 2)
    middle = lax.rem(3 * me + 2, 5)
    for peer in (far, middle, groups * (groups - 1) // 2 - me - far - middle):
        step = lax.rem(peer - me + groups, groups)
        for part, (source, target) in enumerate(
            ((src_ref.at[:, pl.ds(pl.multiple_of(peer * width, 128), width)], landing), (score_ref, score_in))
        ):
            copy = pltpu.make_async_remote_copy(
                src_ref=source,
                dst_ref=target.at[step],
                send_sem=send_sem.at[step, part],
                recv_sem=recv_sem.at[step, part],
                device_id=(home, peer),
                device_id_type=MESH_IDS,
            )
            copy.start()
            copies.append(copy)
    mirror = pltpu.make_async_remote_copy(
        src_ref=grads_ref,
        dst_ref=mirror_out,
        send_sem=mirror_sem.at[0],
        recv_sem=mirror_sem.at[1],
        device_id=(home, groups - 1 - me),
        device_id_type=MESH_IDS,
    )
    mirror.start()
    copies.append(mirror)
    for copy in copies:
        copy.wait()
    own = pl.multiple_of(me * width, 128)
    block = 64

    def body(i, carry):
        rows = pl.ds(pl.multiple_of(i * block, block), block)
        total = src_ref[rows, pl.ds(own, width)].astype(jnp.float32)
        for step in range(1, groups):
            total = total + landing[step, rows, :].astype(jnp.float32)
        out_ref[rows, :] = total.astype(out_ref.dtype)
        return carry

    lax.fori_loop(0, out_ref.shape[0] // block, body, 0)
    score = score_ref[...]
    for step in range(1, groups):
        score = score + score_in[step]
    score_out[...] = score


def dp_scatter(partial, score, grads, groups):
    rows, full = partial.shape
    width = full // groups
    return pl.pallas_call(
        lambda *refs: dp_scatter_kernel(groups, *refs),
        out_shape=(
            jax.ShapeDtypeStruct((rows, width), partial.dtype),
            jax.ShapeDtypeStruct(score.shape, score.dtype),
            jax.ShapeDtypeStruct(grads.shape, grads.dtype),
        ),
        in_specs=[pl.BlockSpec(memory_space=pltpu.VMEM)] * 3,
        out_specs=tuple(pl.BlockSpec(memory_space=pltpu.VMEM) for _ in range(3)),
        scratch_shapes=[
            pltpu.VMEM((groups, rows, width), partial.dtype),
            pltpu.VMEM((groups,) + score.shape, score.dtype),
            pltpu.SemaphoreType.DMA((groups, 2)),
            pltpu.SemaphoreType.DMA((groups, 2)),
            pltpu.SemaphoreType.DMA((2,)),
        ],
        compiler_params=pltpu.CompilerParams(collective_id=0, has_side_effects=True),
    )(partial, score, grads)


def dp_gather_kernel(groups, width, src_ref, x_ref, dy_ref, local_sem, send_sem, recv_sem):
    me = lax.axis_index("dp")
    home = lax.axis_index("expert")
    barrier = pltpu.get_barrier_semaphore()
    for step in range(1, groups):
        peer = lax.rem(me + step, groups)
        pl.semaphore_signal(barrier, 1, device_id=(home, peer), device_id_type=MESH_IDS)
    pl.semaphore_wait(barrier, groups - 1)
    mine = pl.ds(pl.multiple_of(me * width, 128), width)
    copies = []
    far = (groups - 1) * (1 - me // 2)
    middle = lax.rem(3 * me + 2, 5)
    for peer in (far, middle, groups * (groups - 1) // 2 - me - far - middle):
        step = lax.rem(peer - me + groups, groups)
        for part, dst in enumerate((x_ref, dy_ref)):
            copy = pltpu.make_async_remote_copy(
                src_ref=src_ref.at[:, pl.ds(part * width, width)],
                dst_ref=dst.at[:, mine],
                send_sem=send_sem.at[step, part],
                recv_sem=recv_sem.at[step, part],
                device_id=(home, peer),
                device_id_type=MESH_IDS,
            )
            copy.start()
            copies.append(copy)
    for part, dst in enumerate((x_ref, dy_ref)):
        local = pltpu.make_async_copy(
            src_ref.at[:, pl.ds(part * width, width)], dst.at[:, mine], local_sem.at[part]
        )
        local.start()
        copies.append(local)
    for copy in copies:
        copy.wait()


def dp_gather(chunk, groups, width):
    rows = chunk.shape[0]
    full = jax.ShapeDtypeStruct((rows, groups * width), chunk.dtype)
    return pl.pallas_call(
        lambda *refs: dp_gather_kernel(groups, width, *refs),
        out_shape=(full, full),
        in_specs=[pl.BlockSpec(memory_space=pl.ANY)],
        out_specs=(pl.BlockSpec(memory_space=pl.ANY), pl.BlockSpec(memory_space=pl.ANY)),
        scratch_shapes=[
            pltpu.SemaphoreType.DMA((2,)),
            pltpu.SemaphoreType.DMA((groups, 2)),
            pltpu.SemaphoreType.DMA((groups, 2)),
        ],
        compiler_params=pltpu.CompilerParams(collective_id=2, has_side_effects=True),
    )(chunk)


def from_behind(value, axis, by):
    devices = lax.axis_size(axis)
    return lax.ppermute(value, axis, [(i, (i + by) % devices) for i in range(devices)])


def mirror_swap(value, expert_count, groups):
    half_axis = expert_count // 2
    pairs = [
        (slot * groups + group, ((slot + half_axis) % expert_count) * groups + groups - 1 - group)
        for slot in range(expert_count)
        for group in range(groups)
    ]
    return lax.ppermute(value, ("expert", "dp"), pairs)


def pair_lookup(experts, pair_flags, half_axis):
    match = experts[:, None] % half_axis == jnp.arange(half_axis, dtype=jnp.int32)[None, :]
    return jnp.sum(jnp.where(match, pair_flags[None, :], 0), axis=1)


def shards(tokens, cotangent, gate_weight, up_weight, down_weight, expert_ids, gates, swap_flags):
    expert_count = lax.axis_size("expert")
    half_axis = expert_count // 2
    my_slot = lax.axis_index("expert")
    row_count, model_width = tokens.shape
    routed = expert_ids.shape[1]
    capacity = row_count * routed * 5 // (4 * expert_count)
    groups = lax.axis_size("dp")
    quarter = model_width // groups
    own_flag = pair_lookup(jnp.reshape(my_slot, (1,)), swap_flags, half_axis)[0]
    flat_ids = expert_ids.reshape(-1)
    flipped = pair_lookup(flat_ids, swap_flags, half_axis)
    target = jnp.where(flipped == 1, (flat_ids + half_axis) % expert_count, flat_ids)
    copies = row_count * routed
    onehot = (target[:, None] == jnp.arange(expert_count, dtype=jnp.int32)[None, :]).astype(
        jnp.int32
    )
    earlier = jnp.cumsum(onehot, axis=0) - onehot
    position = jnp.sum(earlier * onehot, axis=1)
    buffer_index = target * capacity + position
    source = jnp.zeros((expert_count * capacity,), jnp.int32)
    source = source.at[buffer_index].set(jnp.arange(copies, dtype=jnp.int32) + 1)
    filled = source > 0
    copy_index = jnp.maximum(source - 1, 0)
    token_index = copy_index // routed
    my_group = lax.axis_index("dp")
    x_part = lax.dynamic_slice_in_dim(tokens, my_group * quarter, quarter, axis=1)
    dy_part = lax.dynamic_slice_in_dim(cotangent, my_group * quarter, quarter, axis=1)
    x_buffer = jnp.where(filled[:, None], x_part[token_index], 0)
    dy_buffer = jnp.where(filled[:, None], dy_part[token_index], 0)
    gate_buffer = jnp.where(filled, gates.reshape(-1)[copy_index], 0)
    gate_cols = jnp.zeros((expert_count * capacity, 128), jnp.bfloat16).at[:, 0].set(gate_buffer)
    outgoing = jnp.concatenate([x_buffer, dy_buffer, gate_cols], axis=1)
    arrived = lax.all_to_all(outgoing, "expert", split_axis=0, concat_axis=0, tiled=True)
    weights = (gate_weight, up_weight, down_weight)
    held, arrived = lax.optimization_barrier((weights, arrived))
    moved = mirror_swap(held, expert_count, groups)
    weights = tuple(
        (jnp.where(own_flag == 1, fresh, stay) for fresh, stay in zip(moved, weights))
    )
    x_rows, dy_rows = dp_gather(arrived, groups, quarter)
    gate_rows = arrived[:, 2 * quarter]
    w_gate = weights[0][0]
    w_up = weights[1][0]
    w_down = weights[2][0]
    contract_last = (((1,), (1,)), ((), ()))
    pre_gate = lax.dot_general(x_rows, w_gate, contract_last, preferred_element_type=jnp.float32)
    pre_up = lax.dot_general(x_rows, w_up, contract_last, preferred_element_type=jnp.float32)
    sigma = jax.nn.sigmoid(pre_gate)
    active = pre_gate * sigma
    hidden = (active * pre_up).astype(jnp.bfloat16)
    back = lax.dot_general(dy_rows, w_down, contract_last, preferred_element_type=jnp.float32)
    score_part = jnp.sum(hidden.astype(jnp.float32) * back, axis=1)
    grad_hidden = gate_rows.astype(jnp.float32)[:, None] * back
    slope = sigma * (1.0 + pre_gate * (1.0 - sigma))
    grad_gate = (grad_hidden * pre_up * slope).astype(jnp.bfloat16)
    grad_up = (grad_hidden * active).astype(jnp.bfloat16)
    input_part = jnp.dot(grad_gate, w_gate, preferred_element_type=jnp.float32)
    input_part = input_part + jnp.dot(grad_up, w_up, preferred_element_type=jnp.float32)
    scaled = gate_rows[:, None] * dy_rows
    contract_rows = (((0,), (0,)), ((), ()))
    computed = (grad_gate, grad_up, hidden)
    slots = capacity * expert_count
    score_tile = jnp.zeros((8 * 128,), jnp.float32).at[:slots].set(score_part).reshape(8, 128)
    share, score_sum, mirrored = dp_scatter(
        input_part.astype(jnp.bfloat16), score_tile, jnp.stack(computed), groups
    )
    mine = tuple(jnp.where(own_flag == 1, mirrored[k], computed[k]) for k in range(3))
    grad_wgate = lax.dot_general(
        mine[0], x_rows, contract_rows, preferred_element_type=jnp.float32
    )
    grad_wup = lax.dot_general(mine[1], x_rows, contract_rows, preferred_element_type=jnp.float32)
    grad_wdown = lax.dot_general(mine[2], scaled, contract_rows, preferred_element_type=jnp.float32)
    score_col = jnp.zeros((slots, 128), jnp.bfloat16).at[:, 0].set(
        score_sum.reshape(-1)[:slots].astype(jnp.bfloat16)
    )
    reduced = jnp.concatenate([share, score_col], axis=1)
    back_rows = lax.all_to_all(reduced, "expert", split_axis=0, concat_axis=0, tiled=True)
    per_copy = back_rows[buffer_index].reshape(row_count, routed, quarter + 128)
    input_grad = jnp.sum(per_copy[:, :, :quarter].astype(jnp.float32), axis=1).astype(jnp.bfloat16)
    gate_grad = per_copy[:, :, quarter]
    gradients = (
        grad_wgate.astype(jnp.bfloat16)[None],
        grad_wup.astype(jnp.bfloat16)[None],
        grad_wdown.astype(jnp.bfloat16)[None],
    )
    return (input_grad, gate_grad, gradients[0], gradients[1], gradients[2])


def solution(mesh):
    placed = (
        P("expert", None),
        P("expert", None),
        P("expert", "dp", None),
        P("expert", "dp", None),
        P("expert", "dp", None),
        P("expert", None),
        P("expert", None),
        P(),
    )
    return jax.shard_map(
        shards,
        mesh=mesh,
        in_specs=placed,
        out_specs=(
            P("expert", "dp"),
            P("expert", None),
            P("expert", "dp", None),
            P("expert", "dp", None),
            P("expert", "dp", None),
        ),
        check_vma=False,
    )
```
